512 devices in a mesh: gx: 64 (over z_lo, y, x), gy: 8 (over z_hi, core).
Axes of the slice: x: 4, y: 8, z: 8 (z_hi: 4, z_lo: 2; z = z_hi * 2 + z_lo), core: 2. Of those that a mesh axis runs over, the one named last changes fastest.
Arguments:
- skip_feature_rows: bfloat16 [1024, 192, 512], P(('gx', 'gy')), may hold values from -6 to 6
- coarse_features: bfloat16 [1024, 192, 512], P(('gx', 'gy')), may hold values from -6 to 6
- cotangent: bfloat16 [1024, 192, 512], P(('gx', 'gy')), may hold values from -16 to 16
- fine_coords: int32 [1024, 3], P(('gx', 'gy')), may hold values from 0 to 3, as said below
- coarse_coords: int32 [1024, 3], P(('gx', 'gy')), may hold values from 0 to 1, as said below
- parents: int32 [1024], P(('gx', 'gy')), may hold values from 0 to 1
- counts: int32 [512], P(('gx', 'gy')), may hold values from 1 to 2
- conv_weight: bfloat16 [192, 27, 192], replicated, may hold values from -0.078125 to 0.078125
- up_weight: bfloat16 [8, 192, 192], replicated, may hold values from -0.4375 to 0.4375
Outputs:
- grad_skip: bfloat16 [1024, 192, 512], P(('gx', 'gy'))
- grad_coarse: bfloat16 [1024, 192, 512], P(('gx', 'gy'))
- grad_conv: float32 [192, 27, 192], P('gy')
The draws below stay inside these ranges and needn't reach their ends.
Inputs may be any that keep to these rules, and one draw needn't show every extreme that they name: `fine_coords`: within one tile the fine slots have distinct coordinates in 0..1, 0..1, 0..3, and each equals 2 coarse_coords of its parent plus a 0/1 offset per axis. `coarse_coords`: within one tile the 2 coarse slots hold each coarse block position of the tile once.
All inputs are finite; a program needn't handle non-finite values.
Results may differ from the reference program's by a relative error of at most 0.013.
Values may be sent and summed in bfloat16 or wider, within the bound.
No kernel may reach another device: no remote copies, remote signals or barrier semaphores. Data moves between devices by JAX's collectives and lax.ppermute only.
A program may use at most 128 MiB of HBM per device.

```python
import jax
import jax.numpy as jnp
from jax import lax

CH = 192
NB = 2
FB_X = 2
FB_Y = 2
FB_Z = 4
NC = 2
SLOTS = 1024
COARSE_SLOT_ALL = 1024
N_GX = 64
N_GY = 8


def geometry(key):
    tile_count = N_GX * N_GY
    tile_keys = jax.random.split(jax.random.fold_in(key, 11), tile_count)
    coarse_y = FB_Y // 2
    coarse_z = FB_Z // 2

    def one_tile(tile_key):
        key_pos, key_par, key_oct = jax.random.split(tile_key, 3)
        position = jax.random.permutation(key_pos, NC).astype(jnp.int32)
        coarse = jnp.stack([position // (coarse_y * coarse_z), position // coarse_z % coarse_y, position % coarse_z], 1)
        parent_ids = jax.random.randint(key_par, (NB,), 0, NC, dtype=jnp.int32)
        octant_ids = jax.random.permutation(key_oct, 8).astype(jnp.int32)[:NB]
        octant = jnp.stack([octant_ids // 4, octant_ids // 2 % 2, octant_ids % 2], 1)
        fine = 2 * coarse[parent_ids] + octant
        return (coarse, fine, parent_ids)
    coarse, fine, parent_ids = jax.vmap(one_tile)(tile_keys)
    return (coarse.reshape(tile_count * NC, 3), fine.reshape(tile_count * NB, 3), parent_ids.reshape(tile_count * NB))


def draw_fine_coords(key, part):
    return geometry(key)[1]


def draw_coarse_coords(key, part):
    return geometry(key)[0]


def draw_parents(key, part):
    return geometry(key)[2]


def draw_counts(key, part):
    tile_count = N_GX * N_GY
    drawn = jax.random.randint(jax.random.fold_in(key, 23), (tile_count,), 1, NB + 1, dtype=jnp.int32)
    return drawn.at[0].set(NB)


def raised(values, own_key, source, target, shards_of, factor):
    owner, partner = [(jnp.arange(values.shape[dim]) // (values.shape[dim] // shards_of)).reshape([-1 if axis == dim else 1 for axis in range(values.ndim)]) for dim in (source, target)]
    chosen = jax.random.permutation(own_key, shards_of)[partner]
    strong = (owner == chosen) | (owner == (partner + shards_of // 2) % shards_of)
    return jnp.where(strong, factor * values, values)


def level_of(stream_key, shape, cuts, low, high):
    def one(dim, shards_of):
        draws = jax.random.uniform(jax.random.fold_in(jax.random.fold_in(stream_key, 6), dim), (shards_of,), jnp.float32, low / len(cuts), high / len(cuts))
        return jnp.repeat(jnp.exp(draws), shape[dim] // shards_of).reshape((-1,) + (1,) * (len(shape) - dim - 1))

    level = one(*cuts[0])
    for cut in cuts[1:]:
        level = level * one(*cut)
    return level


def normal_values(rng, shape, scale, bound, pieces=(), kind=jnp.bfloat16):
    loudness = level_of(rng, shape, pieces, -0.22, 0.18) if pieces else 1.0
    result = jax.random.normal(rng, shape, jnp.float32) * scale * loudness
    return jnp.minimum(jnp.maximum(result, -bound), bound).astype(kind)


def gaussian_with(own_key, extent, deviation, reach, pieces, heavy, held_as=jnp.bfloat16):
    values = deviation * jax.random.normal(own_key, extent, jnp.float32)
    if pieces:
        values = values * level_of(own_key, extent, pieces, -0.22, 0.18)
    return jnp.clip(raised(values, jax.random.fold_in(own_key, 3), *heavy), -reach, reach).astype(held_as)


def setup_inputs(seed: int = 0) -> dict:
    streams_of = jax.random.split(jax.random.key(seed), 10)
    return {
        "skip_feature_rows": normal_values(streams_of[0], (SLOTS, CH, 512), 1.0, 6.0, ((0, 512),)),
        "coarse_features": normal_values(streams_of[1], (COARSE_SLOT_ALL, CH, 512), 1.0, 6.0, ((0, 512),)),
        "cotangent": gaussian_with(streams_of[2], (SLOTS, CH, 512), 1.0, 16.0, ((0, 512),), (0, 1, 64, 4.0)),
        "fine_coords": draw_fine_coords(jax.random.fold_in(streams_of[9], 71), 0),
        "coarse_coords": draw_coarse_coords(jax.random.fold_in(streams_of[9], 71), 0),
        "parents": draw_parents(jax.random.fold_in(streams_of[9], 71), 0),
        "counts": draw_counts(jax.random.fold_in(streams_of[9], 71), 0),
        "conv_weight": normal_values(streams_of[7], (CH, 27, CH), (27 * CH) ** -0.5, 0.078125),
        "up_weight": normal_values(streams_of[8], (8, CH, CH), CH ** -0.5, 0.4375),
    }


def index_tuple(anchor):
    return tuple(jnp.asarray(entry).astype(jnp.int32) for entry in anchor)


def add_into(target, addend, anchor):
    anchor = index_tuple(anchor)
    current = lax.dynamic_slice(target, anchor, addend.shape)
    return lax.dynamic_update_slice(target, current + addend, anchor)


def upsample(coarse_row, octant, up_rows):
    channel_count = coarse_row.shape[0]
    block_cube = coarse_row.reshape(channel_count, 8, 8, 8)
    octant_cube = lax.dynamic_slice(block_cube, index_tuple((0, 4 * octant[0], 4 * octant[1], 4 * octant[2])), (channel_count, 4, 4, 4))
    product = jnp.dot(up_rows.astype(jnp.float32), octant_cube.reshape(channel_count, 64).astype(jnp.float32),
                      precision=lax.Precision.HIGHEST)
    product = product.reshape(2, 2, 2, channel_count, 4, 4, 4).transpose(3, 4, 0, 5, 1, 6, 2)
    return product.reshape(channel_count, 512)


def fold_down(grad_row, up_rows):
    channel_count = grad_row.shape[0]
    regrouped = grad_row.reshape(channel_count, 4, 2, 4, 2, 4, 2).transpose(2, 4, 6, 0, 1, 3, 5).reshape(8 * channel_count, 64)
    return lax.dot_general(up_rows.astype(jnp.float32), regrouped.astype(jnp.float32), (((0,), (0,)), ((), ())),
                           precision=lax.Precision.HIGHEST)


def coarse_gradient(grad_rows, parent_ids, octants, coarse_count, up_rows):
    channel_count = grad_rows.shape[1]
    coarse_total = jnp.zeros((coarse_count, channel_count, 8, 8, 8), jnp.float32)
    for member in range(grad_rows.shape[0]):
        addend = fold_down(grad_rows[member], up_rows).reshape(1, channel_count, 4, 4, 4)
        anchor = (parent_ids[member], 0, 4 * octants[member, 0], 4 * octants[member, 1], 4 * octants[member, 2])
        coarse_total = add_into(coarse_total, addend, anchor)
    return coarse_total.astype(jnp.bfloat16).reshape(coarse_count, channel_count, 512)


def columns(padded, coord, reverse):
    channel_count = padded.shape[0]
    window = lax.dynamic_slice(padded, index_tuple((0, 8 * coord[0], 8 * coord[1], 8 * coord[2])), (channel_count, 10, 10, 10))
    shifted = []
    for step_x in range(3):
        for step_y in range(3):
            for step_z in range(3):
                if reverse:
                    first_x, first_y, first_z = 2 - step_x, 2 - step_y, 2 - step_z
                else:
                    first_x, first_y, first_z = step_x, step_y, step_z
                view = window[:, first_x:first_x + 8, first_y:first_y + 8, first_z:first_z + 8]
                shifted.append(view.reshape(channel_count, 512))
    return jnp.concatenate(shifted, 0)


def forward_slot(hidden_cols, cot_row, occupied, weight_flat):
    pre = jnp.dot(weight_flat.astype(jnp.float32), hidden_cols.astype(jnp.float32), precision=lax.Precision.HIGHEST)
    sigma = jax.nn.sigmoid(pre)
    return (cot_row.astype(jnp.float32) * (sigma * (1.0 + pre * (1.0 - sigma))) * occupied).astype(jnp.bfloat16)


def tile_frame(grid_vals, grid_coords, tile_x, tile_y):
    channel_count = grid_vals.shape[3]
    wide = jnp.zeros((channel_count, 24 * FB_X, 24 * FB_Y, 8 * FB_Z + 2), jnp.bfloat16)
    for shift_x in (-1, 0, 1):
        for shift_y in (-1, 0, 1):
            near_x = tile_x + shift_x
            near_y = tile_y + shift_y
            inside = (near_x >= 0) & (near_x < N_GX) & (near_y >= 0) & (near_y < N_GY)
            clamp_x = jnp.clip(near_x, 0, N_GX - 1)
            clamp_y = jnp.clip(near_y, 0, N_GY - 1)
            features = grid_vals[clamp_x, clamp_y] * inside.astype(jnp.bfloat16)
            placed = grid_coords[clamp_x, clamp_y]
            for member in range(NB):
                anchor = (0, 8 * FB_X * (shift_x + 1) + 8 * placed[member, 0],
                          8 * FB_Y * (shift_y + 1) + 8 * placed[member, 1], 1 + 8 * placed[member, 2])
                wide = add_into(wide, features[member].reshape(channel_count, 8, 8, 8), anchor)
    return wide[:, 8 * FB_X - 1:16 * FB_X + 1, 8 * FB_Y - 1:16 * FB_Y + 1, :]


def reference(skip_feature_rows, coarse_features, cotangent, fine_coords, coarse_coords, parents, counts, conv_weight, up_weight):
    tile_count = N_GX * N_GY
    tile_ids = jnp.arange(tile_count, dtype=jnp.int32)
    slot_ids = jnp.arange(tile_count * NB, dtype=jnp.int32)
    owner_tile = slot_ids // NB
    occupied = (slot_ids % NB < counts[owner_tile]).astype(jnp.float32)
    up_rows = up_weight.reshape(8 * CH, CH)
    parent_rows = (owner_tile * NC + parents).astype(jnp.int32)
    octants = (fine_coords - 2 * coarse_coords[parent_rows]).astype(jnp.int32)
    lifted = jax.vmap(lambda coarse_row, octant: upsample(coarse_row, octant, up_rows))(coarse_features[parent_rows], octants)
    hidden = ((lifted + skip_feature_rows.astype(jnp.float32)) * occupied[:, None, None]).astype(jnp.bfloat16)
    hidden_grid = hidden.reshape(N_GX, N_GY, NB, CH, 512)
    coord_grid = fine_coords.reshape(N_GX, N_GY, NB, 3)
    cot_grid = cotangent.reshape(tile_count, NB, CH, 512)
    occupied_grid = occupied.reshape(tile_count, NB)
    weight_flat = conv_weight.reshape(CH, 27 * CH)
    weight_flipped = jnp.transpose(conv_weight, (2, 1, 0)).reshape(CH, 27 * CH)

    def first_pass(weight_sum, tile):
        tile_x = tile // N_GY
        tile_y = tile % N_GY
        padded = tile_frame(hidden_grid, coord_grid, tile_x, tile_y)
        own_coords = coord_grid[tile_x, tile_y]
        hidden_cols = jax.vmap(lambda coord: columns(padded, coord, False))(own_coords)
        grad_pre = jax.vmap(lambda cols_one, cot_row, flag: forward_slot(cols_one, cot_row, flag, weight_flat))(
            hidden_cols, cot_grid[tile], occupied_grid[tile])
        weight_sum = weight_sum + lax.dot_general(grad_pre.astype(jnp.float32), hidden_cols.astype(jnp.float32),
                                                  (((0, 2), (0, 2)), ((), ())), precision=lax.Precision.HIGHEST)
        return weight_sum, grad_pre

    weight_grad, grad_pre_all = lax.scan(first_pass, jnp.zeros((CH, 27 * CH), jnp.float32), tile_ids)
    pre_grid = grad_pre_all.reshape(N_GX, N_GY, NB, CH, 512)

    def second_pass(tile):
        tile_x = tile // N_GY
        tile_y = tile % N_GY
        padded = tile_frame(pre_grid, coord_grid, tile_x, tile_y)
        gradient_columns = jax.vmap(lambda coord: columns(padded, coord, True))(coord_grid[tile_x, tile_y])
        backprop_total = jnp.einsum('iw,uwm->uim', weight_flipped.astype(jnp.float32), gradient_columns.astype(jnp.float32),
                                    precision=lax.Precision.HIGHEST)
        return (backprop_total * occupied_grid[tile][:, None, None]).astype(jnp.bfloat16)

    grad_skip = lax.map(second_pass, tile_ids)
    grad_coarse = jax.vmap(lambda grad_rows, parent_ids, tile_octants: coarse_gradient(grad_rows, parent_ids, tile_octants, NC, up_rows))(
        grad_skip, parents.reshape(tile_count, NB), octants.reshape(tile_count, NB, 3))
    return (grad_skip.reshape(tile_count * NB, CH, 512), grad_coarse.reshape(tile_count * NC, CH, 512),
            weight_grad.reshape(CH, 27, CH))
```

```python
import jax
import jax.numpy as jnp
from jax import lax
from jax.sharding import PartitionSpec as P

FB_X = 2
FB_Y = 2
FB_Z = 4


def padded_2(block, sides, width):
    for axis, dim in sides:
        count = lax.axis_size(axis)
        forward = [(i, i + 1) for i in range(count - 1)]
        backward = [(target, source) for source, target in forward]
        low = lax.ppermute(
            lax.slice_in_dim(block, block.shape[dim] - width, None, axis=dim), axis, forward
        )
        high = lax.ppermute(lax.slice_in_dim(block, 0, width, axis=dim), axis, backward)
        block = jnp.concatenate([low, block, high], axis=dim)
    return block


def index_tuple(anchor):
    return tuple((jnp.asarray(entry).astype(jnp.int32) for entry in anchor))


def add_into(target, addend, anchor):
    anchor = index_tuple(anchor)
    current = lax.dynamic_slice(target, anchor, addend.shape)
    return lax.dynamic_update_slice(target, current + addend, anchor)


def upsample(coarse_row, octant, up_rows):
    channel_count = coarse_row.shape[0]
    block_cube = coarse_row.reshape(channel_count, 8, 8, 8)
    octant_cube = lax.dynamic_slice(
        block_cube,
        index_tuple((0, 4 * octant[0], 4 * octant[1], 4 * octant[2])),
        (channel_count, 4, 4, 4),
    )
    product = jnp.dot(
        up_rows, octant_cube.reshape(channel_count, 64), preferred_element_type=jnp.float32
    )
    product = product.reshape(2, 2, 2, channel_count, 4, 4, 4).transpose(3, 4, 0, 5, 1, 6, 2)
    return product.reshape(channel_count, 512)


def fold_down(grad_row, up_rows):
    channel_count = grad_row.shape[0]
    regrouped = (
        grad_row.reshape(channel_count, 4, 2, 4, 2, 4, 2)
        .transpose(2, 4, 6, 0, 1, 3, 5)
        .reshape(8 * channel_count, 64)
    )
    return lax.dot_general(
        up_rows, regrouped, (((0,), (0,)), ((), ())), preferred_element_type=jnp.float32
    )


def coarse_gradient(grad_rows, parent_ids, octants, coarse_count, up_rows):
    channel_count = grad_rows.shape[1]
    coarse_total = jnp.zeros((coarse_count, channel_count, 8, 8, 8), jnp.float32)
    for member in range(grad_rows.shape[0]):
        addend = fold_down(grad_rows[member], up_rows).reshape(1, channel_count, 4, 4, 4)
        anchor = (
            parent_ids[member],
            0,
            4 * octants[member, 0],
            4 * octants[member, 1],
            4 * octants[member, 2],
        )
        coarse_total = add_into(coarse_total, addend, anchor)
    return coarse_total.astype(jnp.bfloat16).reshape(coarse_count, channel_count, 512)


def columns(padded, coord, reverse):
    channel_count = padded.shape[0]
    window = lax.dynamic_slice(
        padded,
        index_tuple((0, 8 * coord[0], 8 * coord[1], 8 * coord[2])),
        (channel_count, 10, 10, 10),
    )
    shifted = []
    for step_x in range(3):
        for step_y in range(3):
            for step_z in range(3):
                if reverse:
                    first_x, first_y, first_z = (2 - step_x, 2 - step_y, 2 - step_z)
                else:
                    first_x, first_y, first_z = (step_x, step_y, step_z)
                view = window[
                    :, first_x : first_x + 8, first_y : first_y + 8, first_z : first_z + 8
                ]
                shifted.append(view.reshape(channel_count, 512))
    return jnp.concatenate(shifted, 0)


def forward_slot(hidden_cols, cot_row, occupied, weight_flat):
    pre = jnp.dot(weight_flat, hidden_cols, preferred_element_type=jnp.float32)
    sigma = jax.nn.sigmoid(pre)
    return (cot_row.astype(jnp.float32) * (sigma * (1.0 + pre * (1.0 - sigma))) * occupied).astype(
        jnp.bfloat16
    )


def dense_volume(features, coords):
    channel_count = features.shape[1]
    volume = jnp.zeros((channel_count, 8 * FB_X, 8 * FB_Y, 8 * FB_Z), jnp.bfloat16)
    for member in range(features.shape[0]):
        anchor = index_tuple(
            (0, 8 * coords[member, 0], 8 * coords[member, 1], 8 * coords[member, 2])
        )
        volume = lax.dynamic_update_slice(
            volume, features[member].reshape(channel_count, 8, 8, 8), anchor
        )
    return volume


def pad_depth(volume):
    return jnp.pad(volume, ((0, 0), (0, 0), (0, 0), (1, 1)))


XS, YS, ZL, ZH, CORES = 4, 8, 2, 4, 2
PAD_LANES = 1408


def gx_pairs(move):
    pairs = []
    for low in range(ZL):
        for row in range(YS):
            for col in range(XS):
                to_low, to_row, to_col = move(low, row, col)
                pairs.append(((low * YS + row) * XS + col, (to_low * YS + to_row) * XS + to_col))
    return pairs


def gy_pairs(move):
    pairs = []
    for high in range(ZH):
        for core in range(CORES):
            to_high, to_core = move(high, core)
            pairs.append((high * CORES + core, to_high * CORES + to_core))
    return pairs


def pick(array, index, axis):
    return lax.dynamic_index_in_dim(array, index, axis, keepdims=False)


def wire(array, axis, pairs):
    return lax.ppermute(array.astype(jnp.bfloat16), axis, pairs)


def reduce_grad(local_grad):
    rows = local_grad.shape[0]
    part = rows // (ZH * CORES)
    gx = lax.axis_index("gx")
    gy = lax.axis_index("gy")
    core, high = gy % CORES, gy // CORES
    col, row = gx % XS, (gx // XS) % YS
    total = local_grad.shape[1]
    padded = jnp.pad(local_grad, ((0, 0), (0, XS * PAD_LANES - total)))
    split = padded.reshape(ZH, CORES, part, XS * PAD_LANES)
    held = pick(split, core, 1) + wire(
        pick(split, 1 - core, 1), "gy", gy_pairs(lambda h, c: (h, 1 - c))
    ).astype(jnp.float32)
    def lanes_of(array, index):
        return lax.dynamic_slice_in_dim(array, index * PAD_LANES, PAD_LANES, axis=2)

    arrived = []
    for step in (1, 3, 2):
        piece = lanes_of(held, (col + step) % XS)
        arrived.append(wire(piece, "gx", gx_pairs(lambda l, r, c, s=step: (l, r, (c + s) % XS))))
    held = lanes_of(held, col)
    for piece in arrived:
        held = held + piece.astype(jnp.float32)
    held = held.reshape(ZH, part // YS, 2, 2, 2, PAD_LANES)
    for bit, axis in ((0, 4), (1, 3), (2, 2)):
        mine = (row >> bit) & 1
        got = wire(
            pick(held, 1 - mine, axis),
            "gx",
            gx_pairs(lambda l, r, c, b=bit: (l, r ^ (1 << b), c)),
        )
        held = pick(held, mine, axis) + got.astype(jnp.float32)
    arrived = []
    for step in (1, 3, 2):
        piece = pick(held, (high + step) % ZH, 0)
        arrived.append(wire(piece, "gy", gy_pairs(lambda h, c, s=step: ((h + s) % ZH, c))))
    held = pick(held, high, 0)
    for piece in arrived:
        held = held + piece.astype(jnp.float32)
    mine = held.astype(jnp.bfloat16)
    other = wire(mine, "gx", gx_pairs(lambda l, r, c: (1 - l, r, c)))
    held = (mine.astype(jnp.float32) + other.astype(jnp.float32)).astype(jnp.bfloat16)
    held = held.reshape(part // YS, PAD_LANES)
    for bit in (2, 1, 0):
        mine = ((row >> bit) & 1) == 0
        other = wire(held, "gx", gx_pairs(lambda l, r, c, b=bit: (l, r ^ (1 << b), c)))
        low = jnp.where(mine, held, other)
        high_half = jnp.where(mine, other, held)
        held = jnp.stack([low, high_half], axis=1) if bit == 2 else jnp.stack(
            [low, high_half], axis=held.ndim - 1
        )
    held = held.reshape(part, PAD_LANES)
    pieces = jnp.zeros((part, XS * PAD_LANES), jnp.bfloat16)
    pieces = lax.dynamic_update_slice_in_dim(pieces, held, col * PAD_LANES, axis=1)
    for step in (1, 3, 2):
        other = wire(held, "gx", gx_pairs(lambda l, r, c, s=step: (l, r, (c + s) % XS)))
        pieces = lax.dynamic_update_slice_in_dim(
            pieces, other, ((col - step) % XS) * PAD_LANES, axis=1
        )
    return pieces[:, :total].astype(jnp.float32)


def local(
    skip_feature_rows,
    coarse_features,
    cotangent,
    fine_coords,
    coarse_coords,
    parents,
    counts,
    conv_weight,
    up_weight,
):
    slot_count = skip_feature_rows.shape[0]
    channel_count = skip_feature_rows.shape[1]
    coarse_count = coarse_features.shape[0]
    occupied = (jnp.arange(slot_count, dtype=jnp.int32) < counts[0]).astype(jnp.float32)
    up_rows = up_weight.reshape(8 * channel_count, channel_count)
    octants = fine_coords - 2 * coarse_coords[parents]
    lifted = jnp.stack(
        [
            upsample(coarse_features[parents[member]], octants[member], up_rows)
            for member in range(slot_count)
        ],
        0,
    )
    hidden = ((lifted + skip_feature_rows.astype(jnp.float32)) * occupied[:, None, None]).astype(
        jnp.bfloat16
    )
    hidden_frame = pad_depth(padded_2(dense_volume(hidden, fine_coords), (("gx", 1), ("gy", 2)), 1))
    weight_flat = conv_weight.reshape(channel_count, 27 * channel_count)
    weight_flipped = jnp.transpose(conv_weight, (2, 1, 0)).reshape(
        channel_count, 27 * channel_count
    )
    grad_list = []
    local_grad = jnp.zeros((channel_count, 27 * channel_count), jnp.float32)
    for member in range(slot_count):
        cols_one = columns(hidden_frame, fine_coords[member], False)
        grad_one = forward_slot(cols_one, cotangent[member], occupied[member], weight_flat)
        local_grad = local_grad + lax.dot_general(
            grad_one, cols_one, (((1,), (1,)), ((), ())), preferred_element_type=jnp.float32
        )
        grad_list.append(grad_one)
    grad_pre = jnp.stack(grad_list, 0)
    grad_frame = pad_depth(padded_2(dense_volume(grad_pre, fine_coords), (("gx", 1), ("gy", 2)), 1))
    skip_list = []
    for member in range(slot_count):
        grad_cols = columns(grad_frame, fine_coords[member], True)
        backprop_one = jnp.dot(weight_flipped, grad_cols, preferred_element_type=jnp.float32)
        skip_list.append((backprop_one * occupied[member]).astype(jnp.bfloat16))
    grad_skip = jnp.stack(skip_list, 0)
    grad_coarse = coarse_gradient(grad_skip, parents, octants, coarse_count, up_rows)
    grad_conv = reduce_grad(local_grad)
    return (grad_skip, grad_coarse, grad_conv.reshape(grad_conv.shape[0], 27, channel_count))


def solution(mesh):
    in_specs = (
        P(("gx", "gy"), None, None),
        P(("gx", "gy"), None, None),
        P(("gx", "gy"), None, None),
        P(("gx", "gy"), None),
        P(("gx", "gy"), None),
        P(("gx", "gy")),
        P(("gx", "gy")),
        P(),
        P(),
    )
    out_specs = (P(("gx", "gy"), None, None), P(("gx", "gy"), None, None), P("gy", None, None))
    return jax.shard_map(local, mesh=mesh, in_specs=in_specs, out_specs=out_specs, check_vma=False)
```

```python
import functools

import jax
import jax.numpy as jnp
from jax import lax
from jax.experimental import pallas as pl
from jax.experimental.pallas import tpu as pltpu
from jax.sharding import PartitionSpec as P

CH = 192
META = 16
ROWS = CH + META
VOX = 512
OFFSETS = 27
TAPS = OFFSETS * CH
FACE = 128
SOURCES = 2 * VOX + 2 * FACE + 2 * 2 * FACE
PLANES = 10
ZH, CORES, ZL = 4, 2, 2
GROUP = 64
INTERPRET = False

F32 = jnp.float32
BF16 = jnp.bfloat16


def iota(shape, dim):
    return lax.broadcasted_iota(jnp.int32, shape, dim)


def ones_where(condition):
    return jnp.where(condition, 1.0, 0.0).astype(BF16)


def dot(left, right):
    return jnp.dot(left, right, preferred_element_type=F32)


def dot_nt(left, right):
    return lax.dot_general(left, right, (((1,), (1,)), ((), ())), preferred_element_type=F32)


def slot_scalars(fine, coarse, parents, slot):
    parent = parents[slot]
    position = [fine[slot, axis] for axis in range(3)]
    octant = [fine[slot, axis] - 2 * coarse[parent, axis] for axis in range(3)]
    return parent, position, octant


def occupied_of(counts, slot):
    return jnp.where(slot < counts[0], 1.0, 0.0).astype(F32)


def meta_rows(position):
    voxel = iota((META, VOX), 1)
    row = iota((META, VOX), 0)
    x = 8 * position[0] + (voxel >> 6)
    y = 8 * position[1] + ((voxel >> 3) & 7)
    z = 8 * position[2] + (voxel & 7)
    value = jnp.where(row == 0, x, jnp.where(row == 1, y, jnp.where(row == 2, z, 0)))
    return value.astype(F32).astype(BF16)


def face_columns(block, slot):
    lane = iota((1, 4 * FACE), 1)
    face = lane >> 7
    inner = lane & 63
    x_high = 448 + inner
    y_low = (inner >> 3) * 64 + (inner & 7)
    source = jnp.where(
        face == 0, x_high, jnp.where(face == 1, inner, jnp.where(face == 2, y_low + 56, y_low))
    )
    source = jnp.where(((lane >> 6) & 1) == slot, source, -1)
    return dot(block, ones_where(iota((VOX, 4 * FACE), 0) == source))


def store_faces(faces_ref, total):
    row = iota((ROWS, FACE), 0)
    shifts = ((CH, -16.0), (CH, 16.0), (CH + 1, -16.0), (CH + 1, 16.0))
    for face, (where, shift) in enumerate(shifts):
        part = total[:, face * FACE : (face + 1) * FACE]
        faces_ref[face] = (part + jnp.where(row == where, shift, 0.0)).astype(BF16)


def hidden_kernel(fine, coarse_pos, parents, counts, skip, coarse, up, own, faces, total):
    slot = pl.program_id(0)
    parent, position, octant = slot_scalars(fine, coarse_pos, parents, slot)
    voxel = iota((1, VOX), 1)
    p, q, s = voxel >> 6, (voxel >> 3) & 7, voxel & 7
    code = (
        (4 * octant[0] + (p >> 1)) * 64 + (4 * octant[1] + (q >> 1)) * 8 + 4 * octant[2] + (s >> 1)
    )
    spread = dot(coarse[parent], ones_where(iota((VOX, VOX), 0) == code)).astype(BF16)
    kind = 4 * (p & 1) + 2 * (q & 1) + (s & 1)
    lifted = jnp.zeros((CH, VOX), F32)
    for k in range(8):
        lifted = lifted + dot(up[k], spread * ones_where(kind == k))
    hidden = (lifted + skip[0].astype(F32)) * occupied_of(counts, slot)
    own[slot, 0:CH, :] = hidden.astype(BF16)
    own[slot, CH:ROWS, :] = meta_rows(position)
    columns = face_columns(own[slot], slot)

    @pl.when(slot == 0)
    def _():
        total[...] = columns

    @pl.when(slot == 1)
    def _():
        store_faces(faces, total[...] + columns)


def edges_kernel(faces, from_low, from_high, to_high, to_low):
    row = iota((ROWS, FACE), 0)
    lane = iota((1, FACE), 1)
    inside = lane & 15
    for target, face, edge, shift in ((to_high, 2, 56, -16.0), (to_low, 3, 0, 16.0)):
        source = (inside >> 3) * 64 + edge + (inside & 7)
        first = ones_where(iota((FACE, FACE), 0) == jnp.where(lane < 16, source, -1))
        second = ones_where(
            iota((FACE, FACE), 0) == jnp.where((lane >= 16) & (lane < 32), source, -1)
        )
        value = dot(from_low[...], first) + dot(from_high[...], second)
        value = value + jnp.where(row == CH + 1, shift, 0.0)
        target[:, 0:FACE] = faces[face]
        target[:, FACE : 2 * FACE] = value.astype(BF16)


def gather_sources(source, own, low_x, high_x, low_y, high_y):
    source[:, 0:VOX] = own[0]
    source[:, VOX : 2 * VOX] = own[1]
    start = 2 * VOX
    source[:, start : start + FACE] = low_x[...]
    source[:, start + FACE : start + 2 * FACE] = high_x[...]
    start = start + 2 * FACE
    source[:, start : start + 2 * FACE] = low_y[...]
    source[:, start + 2 * FACE : start + 4 * FACE] = high_y[...]


def fill_taps(source, frame, taps, position):
    meta = source[CH:ROWS, :].astype(F32).astype(jnp.int32)
    x = meta[0:1, :] - 8 * position[0] + 1
    y = meta[1:2, :] - 8 * position[1] + 1
    z = meta[2:3, :] - 8 * position[2] + 1
    near = (x >= 0) & (x < 10) & (y >= 0) & (y < 10) & (z >= 0) & (z < 10)
    code = jnp.where(near, x * 128 + y * 10 + z, -1)
    values = source[0:CH, :]
    for pair in range(PLANES // 2):
        place = ones_where(iota((256, SOURCES), 0) + 256 * pair == code)
        frame[:, 256 * pair : 256 * pair + 256] = dot_nt(values, place).astype(BF16)
    lane = iota((1, 9 * 128), 1)
    shift = lane >> 7
    inner = lane & 127
    step_y = jnp.where(shift >= 6, 2, jnp.where(shift >= 3, 1, 0))
    step_z = shift - 3 * step_y
    origin = (inner >> 6) * 128 + (((inner >> 3) & 7) + step_y) * 10 + (inner & 7) + step_z
    shifts = ones_where(iota((256, 9 * 128), 0) == origin)
    for plane in range(9):
        moved = dot(frame[:, 128 * plane : 128 * plane + 256], shifts).astype(BF16)
        for step_x in range(3):
            rest = plane - step_x
            if rest < 0 or rest % 2 or rest > 6:
                continue
            at = 64 * rest
            for g in range(9):
                row = (step_x * 9 + g) * CH
                taps[row : row + CH, at : at + 128] = moved[:, 128 * g : 128 * g + 128]


def forward_kernel(
    fine, counts, core, own, low_x, high_x, low_y, high_y, cot, weight,
    grad, faces, keep, send, source, frame, taps, total, sums,
):
    slot = pl.program_id(0)
    position = [fine[slot, axis] for axis in range(3)]

    @pl.when(slot == 0)
    def _():
        gather_sources(source, own, low_x, high_x, low_y, high_y)
        sums[...] = jnp.zeros_like(sums)

    fill_taps(source, frame, taps, position)
    occupied = occupied_of(counts, slot)
    for half in range(2):
        at = slice(256 * half, 256 * half + 256)
        pre = dot(weight[...], taps[:, at])
        sigma = jax.nn.sigmoid(pre)
        value = cot[0, :, at].astype(F32) * (sigma * (1.0 + pre * (1.0 - sigma))) * occupied
        grad[slot, 0:CH, at] = value.astype(BF16)
    grad[slot, CH:ROWS, :] = meta_rows(position)
    values = grad[slot, 0:CH, :]
    for start in range(0, TAPS, 512):
        size = min(512, TAPS - start)
        sums[:, start : start + size] += dot_nt(values, taps[start : start + size, :])
    columns = face_columns(grad[slot], slot)

    @pl.when(slot == 0)
    def _():
        total[...] = columns

    @pl.when(slot == 1)
    def _():
        store_faces(faces, total[...] + columns)
        part = CH // (ZH * CORES)
        mine = core[0]
        for high in range(ZH):
            own_start = pl.multiple_of((2 * high + mine) * part, 8)
            other_start = pl.multiple_of((2 * high + 1 - mine) * part, 8)
            keep[high] = sums[pl.ds(own_start, part), :]
            send[high] = sums[pl.ds(other_start, part), :].astype(BF16)


def backward_kernel(
    fine, coarse_pos, parents, counts, own, low_x, high_x, low_y, high_y, weight, up,
    skip_grad, coarse_grad, source, frame, taps,
):
    slot = pl.program_id(0)
    parent, position, octant = slot_scalars(fine, coarse_pos, parents, slot)

    @pl.when(slot == 0)
    def _():
        gather_sources(source, own, low_x, high_x, low_y, high_y)
        coarse_grad[...] = jnp.zeros_like(coarse_grad)

    fill_taps(source, frame, taps, position)
    occupied = occupied_of(counts, slot)
    for half in range(2):
        at = slice(256 * half, 256 * half + 256)
        skip_grad[0, :, at] = (dot(weight[...], taps[:, at]) * occupied).astype(BF16)
    lane = iota((1, 8 * 128), 1)
    kind = lane >> 7
    inner = lane & 127
    voxel = (
        (2 * (inner >> 4) + (kind >> 2)) * 64
        + (2 * ((inner >> 2) & 3) + ((kind >> 1) & 1)) * 8
        + 2 * (inner & 3)
        + (kind & 1)
    )
    voxel = jnp.where(inner < 64, voxel, -1)
    grouped = dot(skip_grad[0], ones_where(iota((VOX, 8 * 128), 0) == voxel)).astype(BF16)
    folded = jnp.zeros((CH, 128), F32)
    for k in range(8):
        folded = folded + dot(up[k], grouped[:, 128 * k : 128 * k + 128])
    cell = iota((1, VOX), 1)
    p, q, s = cell >> 6, (cell >> 3) & 7, cell & 7
    inside = ((p >> 2) == octant[0]) & ((q >> 2) == octant[1]) & ((s >> 2) == octant[2])
    code = jnp.where(inside, (p & 3) * 16 + (q & 3) * 4 + (s & 3), -1)
    placed = dot(folded.astype(BF16), ones_where(iota((128, VOX), 0) == code))
    coarse_grad[parent] = (coarse_grad[parent].astype(F32) + placed).astype(BF16)


SMEM = pl.BlockSpec(memory_space=pltpu.SMEM)


def whole(*shape):
    return pl.BlockSpec(shape, lambda slot: (0,) * len(shape))


def one_slot(*shape):
    return pl.BlockSpec((1,) + shape, lambda slot: (slot,) + (0,) * len(shape))


def shaped(shape, kind=BF16):
    return jax.ShapeDtypeStruct(shape, kind)


def cost(flops, moved):
    return pl.CostEstimate(flops=flops, bytes_accessed=moved, transcendentals=0)


SOURCE_SPECS = [
    whole(2, ROWS, VOX),
    whole(ROWS, FACE),
    whole(ROWS, FACE),
    whole(ROWS, 2 * FACE),
    whole(ROWS, 2 * FACE),
]
TAP_SCRATCH = [
    pltpu.VMEM((ROWS, SOURCES), BF16),
    pltpu.VMEM((CH, 128 * PLANES), BF16),
    pltpu.VMEM((TAPS, VOX), BF16),
]


def make_hidden(fine, coarse_pos, parents, counts, skip, coarse, up):
    return pl.pallas_call(
        hidden_kernel,
        grid=(2,),
        in_specs=[SMEM] * 4
        + [one_slot(CH, VOX), whole(2, CH, VOX), whole(8, CH, CH)],
        out_specs=[whole(2, ROWS, VOX), whole(4, ROWS, FACE)],
        out_shape=[shaped((2, ROWS, VOX)), shaped((4, ROWS, FACE))],
        scratch_shapes=[pltpu.VMEM((ROWS, 4 * FACE), F32)],
        cost_estimate=cost(2_000_000_000, 3_000_000),
        interpret=INTERPRET,
        name="hidden",
    )(fine, coarse_pos, parents, counts, skip, coarse, up)


def exchange(own, faces):
    def both(axis, to_high, to_low):
        count = lax.axis_size(axis)
        forward = [(i, i + 1) for i in range(count - 1)]
        backward = [(target, source) for source, target in forward]
        return lax.ppermute(to_high, axis, forward), lax.ppermute(to_low, axis, backward)

    low_x, high_x = both("gx", faces[0], faces[1])
    to_high, to_low = pl.pallas_call(
        edges_kernel,
        out_shape=[shaped((ROWS, 2 * FACE))] * 2,
        interpret=INTERPRET,
        name="edges",
    )(faces, low_x, high_x)
    low_y, high_y = both("gy", to_high, to_low)
    return own, low_x, high_x, low_y, high_y


def run_forward(fine, counts, core, sources, cot, weight):
    part = CH // (ZH * CORES)
    return pl.pallas_call(
        forward_kernel,
        grid=(2,),
        in_specs=[SMEM] * 3 + SOURCE_SPECS + [one_slot(CH, VOX), whole(CH, TAPS)],
        out_specs=[
            whole(2, ROWS, VOX),
            whole(4, ROWS, FACE),
            whole(ZH, part, TAPS),
            whole(ZH, part, TAPS),
        ],
        out_shape=[
            shaped((2, ROWS, VOX)),
            shaped((4, ROWS, FACE)),
            shaped((ZH, part, TAPS), F32),
            shaped((ZH, part, TAPS)),
        ],
        scratch_shapes=TAP_SCRATCH
        + [pltpu.VMEM((ROWS, 4 * FACE), F32), pltpu.VMEM((CH, TAPS), F32)],
        cost_estimate=cost(8_000_000_000, 8_000_000),
        interpret=INTERPRET,
        name="forward",
    )(fine, counts, core, *sources, cot, weight)


def run_backward(fine, coarse_pos, parents, counts, sources, weight, up):
    return pl.pallas_call(
        backward_kernel,
        grid=(2,),
        in_specs=[SMEM] * 4 + SOURCE_SPECS + [whole(CH, TAPS), whole(8, CH, CH)],
        out_specs=[one_slot(CH, VOX), whole(2, CH, VOX)],
        out_shape=[shaped((2, CH, VOX)), shaped((2, CH, VOX))],
        scratch_shapes=TAP_SCRATCH,
        cost_estimate=cost(6_000_000_000, 4_000_000),
        interpret=INTERPRET,
        name="backward",
    )(fine, coarse_pos, parents, counts, *sources, weight, up)


def gy_pairs(move):
    pairs = []
    for high in range(ZH):
        for core in range(CORES):
            to_high, to_core = move(high, core)
            pairs.append((high * CORES + core, to_high * CORES + to_core))
    return pairs


def pick(array, index):
    return lax.dynamic_index_in_dim(array, index, 0, keepdims=False)


def reduce_grad(keep, send):
    high = lax.axis_index("gy") // CORES
    other = lax.ppermute(send, "gy", gy_pairs(lambda h, c: (h, 1 - c)))
    held = keep + other.astype(F32)
    arrived = []
    for step in (1, 3, 2):
        piece = pick(held, (high + step) % ZH).astype(BF16)
        arrived.append(
            lax.ppermute(piece, "gy", gy_pairs(lambda h, c, s=step: ((h + s) % ZH, c)))
        )
    held = pick(held, high)
    for piece in arrived:
        held = held + piece.astype(F32)
    part, taps = held.shape
    pieces = held.astype(BF16).reshape(GROUP, part * taps // GROUP)
    pieces = lax.all_to_all(pieces, "gx", 0, 0, tiled=True)
    mine = jnp.sum(pieces.astype(F32), axis=0, keepdims=True).astype(BF16)
    spread = jnp.broadcast_to(mine, pieces.shape)
    return lax.all_to_all(spread, "gx", 0, 0, tiled=True).reshape(part, taps).astype(F32)


def local(
    skip_feature_rows,
    coarse_features,
    cotangent,
    fine_coords,
    coarse_coords,
    parents,
    counts,
    conv_weight,
    up_weight,
):
    core = (lax.axis_index("gy") % CORES).astype(jnp.int32).reshape(1)
    weight_flat = conv_weight.reshape(CH, TAPS)
    weight_back = jnp.transpose(conv_weight[:, ::-1, :], (2, 1, 0)).reshape(CH, TAPS)
    up_back = jnp.swapaxes(up_weight, 1, 2)
    own, faces = make_hidden(
        fine_coords, coarse_coords, parents, counts, skip_feature_rows, coarse_features, up_weight
    )
    sources = exchange(own, faces)
    grad, grad_faces, keep, send = run_forward(
        fine_coords, counts, core, sources, cotangent, weight_flat
    )
    grad_conv = reduce_grad(keep, send)
    grad_sources = exchange(grad, grad_faces)
    grad_skip, grad_coarse = run_backward(
        fine_coords, coarse_coords, parents, counts, grad_sources, weight_back, up_back
    )
    return (grad_skip, grad_coarse, grad_conv.reshape(grad_conv.shape[0], OFFSETS, CH))


def solution(mesh):
    in_specs = (
        P(("gx", "gy"), None, None),
        P(("gx", "gy"), None, None),
        P(("gx", "gy"), None, None),
        P(("gx", "gy"), None),
        P(("gx", "gy"), None),
        P(("gx", "gy")),
        P(("gx", "gy")),
        P(),
        P(),
    )
    out_specs = (P(("gx", "gy"), None, None), P(("gx", "gy"), None, None), P("gy", None, None))
    return jax.shard_map(local, mesh=mesh, in_specs=in_specs, out_specs=out_specs, check_vma=False)
```

```python
import jax
import jax.numpy as jnp
from jax import lax
from jax.experimental import pallas as pl
from jax.experimental.pallas import tpu as pltpu
from jax.sharding import PartitionSpec as P


CH = 192
META = 16
ROWS = CH + META
VOX = 512
OFFSETS = 27
TAPS = OFFSETS * CH
TILES = 41
PADDED = 128 * TILES
FACE = 128
SOURCES = 2 * VOX + 2 * FACE + 2 * 2 * FACE
PLANES = 10
ZH, CORES = 4, 2
GROUP = 64
SMALL = 24 * 1024 * 1024
INTERPRET = False

F32 = jnp.float32
BF16 = jnp.bfloat16


def iota(shape, dim):
    return lax.broadcasted_iota(jnp.int32, shape, dim)


def ones_where(condition):
    return jnp.where(condition, 1.0, 0.0).astype(BF16)


def dot(left, right):
    return jnp.dot(left, right, preferred_element_type=F32)


def dot_nt(left, right):
    return lax.dot_general(left, right, (((1,), (1,)), ((), ())), preferred_element_type=F32)


def slot_scalars(fine, coarse, parents, slot):
    parent = parents[slot]
    position = [fine[slot, axis] for axis in range(3)]
    octant = [fine[slot, axis] - 2 * coarse[parent, axis] for axis in range(3)]
    return parent, position, octant


def occupied_of(counts, slot):
    return jnp.where(slot < counts[0], 1.0, 0.0).astype(F32)


def meta_rows(position):
    voxel = iota((META, VOX), 1)
    row = iota((META, VOX), 0)
    x = 8 * position[0] + (voxel >> 6)
    y = 8 * position[1] + ((voxel >> 3) & 7)
    z = 8 * position[2] + (voxel & 7)
    value = jnp.where(row == 0, x, jnp.where(row == 1, y, jnp.where(row == 2, z, 0)))
    return value.astype(F32).astype(BF16)


def face_columns(block, slot):
    lane = iota((1, 4 * FACE), 1)
    face = lane >> 7
    inner = lane & 63
    x_high = 448 + inner
    y_low = (inner >> 3) * 64 + (inner & 7)
    source = jnp.where(
        face == 0, x_high, jnp.where(face == 1, inner, jnp.where(face == 2, y_low + 56, y_low))
    )
    source = jnp.where(((lane >> 6) & 1) == slot, source, -1)
    return dot(block, ones_where(iota((VOX, 4 * FACE), 0) == source))


def store_faces(faces_ref, total):
    row = iota((ROWS, FACE), 0)
    shifts = ((CH, -16.0), (CH, 16.0), (CH + 1, -16.0), (CH + 1, 16.0))
    for face, (where, shift) in enumerate(shifts):
        part = total[:, face * FACE : (face + 1) * FACE]
        faces_ref[face] = (part + jnp.where(row == where, shift, 0.0)).astype(BF16)


def hidden_kernel(fine, coarse_pos, parents, counts, skip, coarse, up, own, faces, total):
    slot = pl.program_id(0)
    parent, position, octant = slot_scalars(fine, coarse_pos, parents, slot)
    voxel = iota((1, VOX), 1)
    p, q, s = voxel >> 6, (voxel >> 3) & 7, voxel & 7
    code = (
        (4 * octant[0] + (p >> 1)) * 64 + (4 * octant[1] + (q >> 1)) * 8 + 4 * octant[2] + (s >> 1)
    )
    spread = dot(coarse[parent], ones_where(iota((VOX, VOX), 0) == code)).astype(BF16)
    kind = 4 * (p & 1) + 2 * (q & 1) + (s & 1)
    lifted = jnp.zeros((CH, VOX), F32)
    for k in range(8):
        lifted = lifted + dot(up[k], spread * ones_where(kind == k))
    hidden = (lifted + skip[0].astype(F32)) * occupied_of(counts, slot)
    own[slot, 0:CH, :] = hidden.astype(BF16)
    own[slot, CH:ROWS, :] = meta_rows(position)
    columns = face_columns(own[slot], slot)

    @pl.when(slot == 0)
    def _():
        total[...] = columns

    @pl.when(slot == 1)
    def _():
        store_faces(faces, total[...] + columns)


def edges_kernel(faces, from_low, from_high, to_high, to_low):
    row = iota((ROWS, FACE), 0)
    lane = iota((1, FACE), 1)
    inside = lane & 15
    for target, face, edge, shift in ((to_high, 2, 56, -16.0), (to_low, 3, 0, 16.0)):
        source = (inside >> 3) * 64 + edge + (inside & 7)
        first = ones_where(iota((FACE, FACE), 0) == jnp.where(lane < 16, source, -1))
        second = ones_where(
            iota((FACE, FACE), 0) == jnp.where((lane >= 16) & (lane < 32), source, -1)
        )
        value = dot(from_low[...], first) + dot(from_high[...], second)
        value = value + jnp.where(row == CH + 1, shift, 0.0)
        target[:, 0:FACE] = faces[face]
        target[:, FACE : 2 * FACE] = value.astype(BF16)


def gather_sources(source, own, low_x, high_x, low_y, high_y):
    source[:, 0:VOX] = own[0]
    source[:, VOX : 2 * VOX] = own[1]
    start = 2 * VOX
    source[:, start : start + FACE] = low_x[...]
    source[:, start + FACE : start + 2 * FACE] = high_x[...]
    start = start + 2 * FACE
    source[:, start : start + 2 * FACE] = low_y[...]
    source[:, start + 2 * FACE : start + 4 * FACE] = high_y[...]


def fill_taps(source, frame, taps, position):
    meta = source[CH:ROWS, :].astype(F32).astype(jnp.int32)
    x = meta[0:1, :] - 8 * position[0] + 1
    y = meta[1:2, :] - 8 * position[1] + 1
    z = meta[2:3, :] - 8 * position[2] + 1
    near = (x >= 0) & (x < 10) & (y >= 0) & (y < 10) & (z >= 0) & (z < 10)
    code = jnp.where(near, x * 128 + y * 10 + z, -1)
    values = source[0:CH, :]
    for pair in range(PLANES // 2):
        place = ones_where(iota((256, SOURCES), 0) + 256 * pair == code)
        frame[:, 256 * pair : 256 * pair + 256] = dot_nt(values, place).astype(BF16)
    lane = iota((1, 9 * 128), 1)
    shift = lane >> 7
    inner = lane & 127
    step_y = jnp.where(shift >= 6, 2, jnp.where(shift >= 3, 1, 0))
    step_z = shift - 3 * step_y
    origin = (inner >> 6) * 128 + (((inner >> 3) & 7) + step_y) * 10 + (inner & 7) + step_z
    shifts = ones_where(iota((256, 9 * 128), 0) == origin)
    for plane in range(9):
        moved = dot(frame[:, 128 * plane : 128 * plane + 256], shifts).astype(BF16)
        for step_x in range(3):
            rest = plane - step_x
            if rest < 0 or rest % 2 or rest > 6:
                continue
            at = 64 * rest
            for g in range(9):
                row = (step_x * 9 + g) * CH
                taps[row : row + CH, at : at + 128] = moved[:, 128 * g : 128 * g + 128]


def forward_kernel(
    fine, counts, core, own, low_x, high_x, low_y, high_y, cot, weight,
    grad, faces, keep, send, source, frame, taps, total, sums,
):
    slot = pl.program_id(0)
    position = [fine[slot, axis] for axis in range(3)]

    @pl.when(slot == 0)
    def _():
        gather_sources(source, own, low_x, high_x, low_y, high_y)
        sums[...] = jnp.zeros_like(sums)

    fill_taps(source, frame, taps, position)
    occupied = occupied_of(counts, slot)
    for half in range(2):
        at = slice(256 * half, 256 * half + 256)
        pre = dot(weight[...], taps[:, at])
        sigma = jax.nn.sigmoid(pre)
        value = cot[0, :, at].astype(F32) * (sigma * (1.0 + pre * (1.0 - sigma))) * occupied
        grad[slot, 0:CH, at] = value.astype(BF16)
    grad[slot, CH:ROWS, :] = meta_rows(position)
    values = grad[slot, 0:CH, :]
    for start in range(0, TAPS, 512):
        size = min(512, TAPS - start)
        sums[:, start : start + size] += dot_nt(values, taps[start : start + size, :])
    columns = face_columns(grad[slot], slot)

    @pl.when(slot == 0)
    def _():
        total[...] = columns

    @pl.when(slot == 1)
    def _():
        store_faces(faces, total[...] + columns)
        part = CH // (ZH * CORES)
        mine = core[0]
        for high in range(ZH):
            own_start = pl.multiple_of((2 * high + mine) * part, 8)
            other_start = pl.multiple_of((2 * high + 1 - mine) * part, 8)
            keep[high] = sums[pl.ds(own_start, part), :]
            send[high] = sums[pl.ds(other_start, part), :].astype(BF16)


def backward_kernel(
    fine, coarse_pos, parents, counts, own, low_x, high_x, low_y, high_y, weight, up,
    skip_grad, coarse_grad, source, frame, taps,
):
    slot = pl.program_id(0)
    parent, position, octant = slot_scalars(fine, coarse_pos, parents, slot)

    @pl.when(slot == 0)
    def _():
        gather_sources(source, own, low_x, high_x, low_y, high_y)
        coarse_grad[...] = jnp.zeros_like(coarse_grad)

    fill_taps(source, frame, taps, position)
    occupied = occupied_of(counts, slot)
    for half in range(2):
        at = slice(256 * half, 256 * half + 256)
        skip_grad[0, :, at] = (dot(weight[...], taps[:, at]) * occupied).astype(BF16)
    lane = iota((1, 8 * 128), 1)
    kind = lane >> 7
    inner = lane & 127
    voxel = (
        (2 * (inner >> 4) + (kind >> 2)) * 64
        + (2 * ((inner >> 2) & 3) + ((kind >> 1) & 1)) * 8
        + 2 * (inner & 3)
        + (kind & 1)
    )
    voxel = jnp.where(inner < 64, voxel, -1)
    grouped = dot(skip_grad[0], ones_where(iota((VOX, 8 * 128), 0) == voxel)).astype(BF16)
    folded = jnp.zeros((CH, 128), F32)
    for k in range(8):
        folded = folded + dot(up[k], grouped[:, 128 * k : 128 * k + 128])
    cell = iota((1, VOX), 1)
    p, q, s = cell >> 6, (cell >> 3) & 7, cell & 7
    inside = ((p >> 2) == octant[0]) & ((q >> 2) == octant[1]) & ((s >> 2) == octant[2])
    code = jnp.where(inside, (p & 3) * 16 + (q & 3) * 4 + (s & 3), -1)
    placed = dot(folded.astype(BF16), ones_where(iota((128, VOX), 0) == code))
    coarse_grad[parent] = (coarse_grad[parent].astype(F32) + placed).astype(BF16)


def flatten_kernel(weight, flat):
    for pair in range(OFFSETS // 2):
        flat[:, 384 * pair : 384 * pair + 384] = jnp.concatenate(
            [weight[2 * pair], weight[2 * pair + 1]], axis=1
        )
    flat[:, TAPS - CH : TAPS] = weight[OFFSETS - 1]


def flatten_back_kernel(weight, up, flat, up_back):
    last = OFFSETS - 1
    for pair in range(OFFSETS // 2):
        flat[:, 384 * pair : 384 * pair + 384] = jnp.concatenate(
            [weight[last - 2 * pair].T, weight[last - 2 * pair - 1].T], axis=1
        )
    flat[:, TAPS - CH : TAPS] = weight[0].T
    for k in range(8):
        up_back[k] = up[k].T


def pack_kernel(own, first, second, third, packed):
    def tile(index):
        at = slice(128 * index, 128 * index + 128)
        value = own[:, at]
        for piece in (first, second, third):
            value = value + piece[:, at].astype(F32)
        return value

    part = own.shape[0]
    for pair in range(TILES // 2):
        both = jnp.concatenate([tile(2 * pair), tile(2 * pair + 1)], axis=0)
        packed[2 * part * pair : 2 * part * pair + 2 * part, :] = both.astype(BF16)
    start = part * (TILES - 1)
    rest = packed.shape[0] - start - part
    tail = jnp.concatenate([tile(TILES - 1), jnp.zeros((rest, 128), F32)], axis=0)
    packed[start:, :] = tail.astype(BF16)


def total_kernel(pieces, spread):
    total = jnp.sum(pieces[...].astype(F32), axis=0, keepdims=True).astype(BF16)
    spread[...] = jnp.broadcast_to(total, spread.shape)


def unpack_kernel(packed, out):
    part = out.shape[1]

    def tiles(index):
        both = packed[2 * part * index : 2 * part * index + 2 * part, :].astype(F32)
        return both[0:part], both[part : 2 * part]

    loaded = []
    for index in range(TILES // 2):
        loaded.extend(tiles(index))
    start = part * (TILES - 1)
    loaded.append(packed[start : start + 2 * part - 8 - 8, :].astype(F32)[0:part])
    for pair in range(OFFSETS // 2):
        wide = jnp.concatenate(loaded[3 * pair : 3 * pair + 3], axis=1)
        out[2 * pair] = wide[:, 0:CH]
        out[2 * pair + 1] = wide[:, CH : 2 * CH]
    wide = jnp.concatenate(loaded[TILES - 2 : TILES], axis=1)
    out[OFFSETS - 1] = wide[:, 0:CH]


SMEM = pl.BlockSpec(memory_space=pltpu.SMEM)


def whole(*shape):
    return pl.BlockSpec(shape, lambda slot: (0,) * len(shape))


def one_slot(*shape):
    return pl.BlockSpec((1,) + shape, lambda slot: (slot,) + (0,) * len(shape))


def shaped(shape, kind=BF16):
    return jax.ShapeDtypeStruct(shape, kind)


def cost(flops, moved):
    return pl.CostEstimate(flops=flops, bytes_accessed=moved, transcendentals=0)


SOURCE_SPECS = [
    whole(2, ROWS, VOX),
    whole(ROWS, FACE),
    whole(ROWS, FACE),
    whole(ROWS, 2 * FACE),
    whole(ROWS, 2 * FACE),
]
TAP_SCRATCH = [
    pltpu.VMEM((ROWS, SOURCES), BF16),
    pltpu.VMEM((CH, 128 * PLANES), BF16),
    pltpu.VMEM((TAPS, VOX), BF16),
]


def make_hidden(fine, coarse_pos, parents, counts, skip, coarse, up):
    return pl.pallas_call(
        hidden_kernel,
        grid=(2,),
        in_specs=[SMEM] * 4
        + [one_slot(CH, VOX), whole(2, CH, VOX), whole(8, CH, CH)],
        out_specs=[whole(2, ROWS, VOX), whole(4, ROWS, FACE)],
        out_shape=[shaped((2, ROWS, VOX)), shaped((4, ROWS, FACE))],
        scratch_shapes=[pltpu.VMEM((ROWS, 4 * FACE), F32)],
        cost_estimate=cost(2_000_000_000, 3_000_000),
        interpret=INTERPRET,
        name="hidden",
    )(fine, coarse_pos, parents, counts, skip, coarse, up)


def small_kernel(body, outs, vmem=None):
    return pl.pallas_call(
        body,
        out_shape=outs,
        compiler_params=pltpu.CompilerParams(vmem_limit_bytes=vmem),
        cost_estimate=cost(1_000_000, 3_000_000),
        interpret=INTERPRET,
    )


def both_ways(axis, to_high, to_low):
    count = lax.axis_size(axis)
    forward = [(i, i + 1) for i in range(count - 1)]
    backward = [(target, source) for source, target in forward]
    return lax.ppermute(to_high, axis, forward), lax.ppermute(to_low, axis, backward)


def exchange(own, faces, beside_x=()):
    low_x, high_x = both_ways("gx", faces[0], faces[1])
    low_x, high_x, beside_x = lax.optimization_barrier((low_x, high_x, beside_x))
    to_high, to_low = small_kernel(edges_kernel, [shaped((ROWS, 2 * FACE))] * 2, SMALL)(
        faces, low_x, high_x
    )
    low_y, high_y = both_ways("gy", to_high, to_low)
    return (own, low_x, high_x, low_y, high_y), beside_x


def run_forward(fine, counts, core, sources, cot, weight):
    part = CH // (ZH * CORES)
    return pl.pallas_call(
        forward_kernel,
        grid=(2,),
        in_specs=[SMEM] * 3 + SOURCE_SPECS + [one_slot(CH, VOX), whole(CH, TAPS)],
        out_specs=[
            whole(2, ROWS, VOX),
            whole(4, ROWS, FACE),
            whole(ZH, part, PADDED),
            whole(ZH, part, PADDED),
        ],
        out_shape=[
            shaped((2, ROWS, VOX)),
            shaped((4, ROWS, FACE)),
            shaped((ZH, part, PADDED), F32),
            shaped((ZH, part, PADDED)),
        ],
        scratch_shapes=TAP_SCRATCH
        + [pltpu.VMEM((ROWS, 4 * FACE), F32), pltpu.VMEM((CH, PADDED), F32)],
        cost_estimate=cost(8_000_000_000, 8_000_000),
        interpret=INTERPRET,
        name="forward",
    )(fine, counts, core, *sources, cot, weight)


def run_backward(fine, coarse_pos, parents, counts, sources, weight, up):
    return pl.pallas_call(
        backward_kernel,
        grid=(2,),
        in_specs=[SMEM] * 4 + SOURCE_SPECS + [whole(CH, TAPS), whole(8, CH, CH)],
        out_specs=[one_slot(CH, VOX), whole(2, CH, VOX)],
        out_shape=[shaped((2, CH, VOX)), shaped((2, CH, VOX))],
        scratch_shapes=TAP_SCRATCH,
        cost_estimate=cost(6_000_000_000, 4_000_000),
        interpret=INTERPRET,
        name="backward",
    )(fine, coarse_pos, parents, counts, *sources, weight, up)


def gy_pairs(move):
    pairs = []
    for high in range(ZH):
        for core in range(CORES):
            to_high, to_core = move(high, core)
            pairs.append((high * CORES + core, to_high * CORES + to_core))
    return pairs


def pick(array, index):
    return lax.dynamic_index_in_dim(array, index, 0, keepdims=False)


def reduce_first(keep, send):
    high = lax.axis_index("gy") // CORES
    other = lax.ppermute(send, "gy", gy_pairs(lambda h, c: (h, 1 - c)))
    held = keep + other.astype(F32)
    arrived = []
    for step in (1, 3, 2):
        piece = pick(held, (high + step) % ZH).astype(BF16)
        arrived.append(lax.ppermute(piece, "gy", gy_pairs(lambda h, c, s=step: ((h + s) % ZH, c))))
    return (pick(held, high), *arrived)


def reduce_second(terms):
    packed = small_kernel(pack_kernel, shaped((GROUP * 16, 128)), SMALL)(*terms)
    pieces = lax.all_to_all(packed.reshape(GROUP, 16, 128), "gx", 0, 0, tiled=True)
    spread = small_kernel(total_kernel, shaped((GROUP, 16, 128)), SMALL)(pieces)
    packed = lax.all_to_all(spread, "gx", 0, 0, tiled=True).reshape(GROUP * 16, 128)
    part = terms[0].shape[0]
    return small_kernel(unpack_kernel, shaped((OFFSETS, part, CH), F32), SMALL)(packed)


def local(
    skip_feature_rows,
    coarse_features,
    cotangent,
    fine_coords,
    coarse_coords,
    parents,
    counts,
    conv_weight,
    up_weight,
):
    core = (lax.axis_index("gy") % CORES).astype(jnp.int32).reshape(1)
    by_offset = jnp.transpose(conv_weight, (1, 0, 2))
    weight_flat = small_kernel(flatten_kernel, shaped((CH, TAPS)))(by_offset)
    backs = small_kernel(
        flatten_back_kernel, [shaped((CH, TAPS)), shaped((8, CH, CH))]
    )(by_offset, up_weight)
    own, faces = make_hidden(
        fine_coords, coarse_coords, parents, counts, skip_feature_rows, coarse_features, up_weight
    )
    sources, (weight_back, up_back) = exchange(own, faces, tuple(backs))
    grad, grad_faces, keep, send = run_forward(
        fine_coords, counts, core, sources, cotangent, weight_flat
    )
    terms = reduce_first(keep, send)
    grad_sources, _ = exchange(grad, grad_faces)
    grad_skip, grad_coarse = run_backward(
        fine_coords, coarse_coords, parents, counts, grad_sources, weight_back, up_back
    )
    terms, grad_skip = lax.optimization_barrier((terms, grad_skip))
    grad_conv = reduce_second(terms)
    return (grad_skip, grad_coarse, jnp.transpose(grad_conv, (1, 0, 2)))


def solution(mesh):
    in_specs = (
        P(("gx", "gy"), None, None),
        P(("gx", "gy"), None, None),
        P(("gx", "gy"), None, None),
        P(("gx", "gy"), None),
        P(("gx", "gy"), None),
        P(("gx", "gy")),
        P(("gx", "gy")),
        P(),
        P(),
    )
    out_specs = (P(("gx", "gy"), None, None), P(("gx", "gy"), None, None), P("gy", None, None))
    return jax.shard_map(local, mesh=mesh, in_specs=in_specs, out_specs=out_specs, check_vma=False)
```

```python
import jax
import jax.numpy as jnp
from jax import lax
from jax.experimental import pallas as pl
from jax.experimental.pallas import tpu as pltpu
from jax.sharding import PartitionSpec as P


CH = 192
META = 16
ROWS = CH + META
VOX = 512
OFFSETS = 27
TAPS = OFFSETS * CH
TILES = 41
PADDED = 128 * TILES
FACE = 128
SOURCES = 2 * VOX + 2 * FACE + 2 * 2 * FACE
PLANES = 10
ZH, CORES, ZL = 4, 2, 2
GROUP, SIDE, XS = 64, 8, 4
SMALL = 24 * 1024 * 1024
INTERPRET = False

F32 = jnp.float32
BF16 = jnp.bfloat16


def iota(shape, dim):
    return lax.broadcasted_iota(jnp.int32, shape, dim)


def ones_where(condition):
    return jnp.where(condition, 1.0, 0.0).astype(BF16)


def dot(left, right):
    return jnp.dot(left, right, preferred_element_type=F32)


def dot_nt(left, right):
    return lax.dot_general(left, right, (((1,), (1,)), ((), ())), preferred_element_type=F32)


def slot_scalars(fine, coarse, parents, slot):
    parent = parents[slot]
    position = [fine[slot, axis] for axis in range(3)]
    octant = [fine[slot, axis] - 2 * coarse[parent, axis] for axis in range(3)]
    return parent, position, octant


def occupied_of(counts, slot):
    return jnp.where(slot < counts[0], 1.0, 0.0).astype(F32)


def meta_rows(position):
    voxel = iota((META, VOX), 1)
    row = iota((META, VOX), 0)
    x = 8 * position[0] + (voxel >> 6)
    y = 8 * position[1] + ((voxel >> 3) & 7)
    z = 8 * position[2] + (voxel & 7)
    value = jnp.where(row == 0, x, jnp.where(row == 1, y, jnp.where(row == 2, z, 0)))
    return value.astype(F32).astype(BF16)


def face_columns(block, slot):
    lane = iota((1, 4 * FACE), 1)
    face = lane >> 7
    inner = lane & 63
    x_high = 448 + inner
    y_low = (inner >> 3) * 64 + (inner & 7)
    source = jnp.where(
        face == 0, x_high, jnp.where(face == 1, inner, jnp.where(face == 2, y_low + 56, y_low))
    )
    source = jnp.where(((lane >> 6) & 1) == slot, source, -1)
    return dot(block, ones_where(iota((VOX, 4 * FACE), 0) == source))


def store_faces(faces_ref, total):
    row = iota((ROWS, FACE), 0)
    shifts = ((CH, -16.0), (CH, 16.0), (CH + 1, -16.0), (CH + 1, 16.0))
    for face, (where, shift) in enumerate(shifts):
        part = total[:, face * FACE : (face + 1) * FACE]
        faces_ref[face] = (part + jnp.where(row == where, shift, 0.0)).astype(BF16)


def hidden_kernel(fine, coarse_pos, parents, counts, skip, coarse, up, own, faces, total):
    slot = pl.program_id(0)
    parent, position, octant = slot_scalars(fine, coarse_pos, parents, slot)
    voxel = iota((1, VOX), 1)
    p, q, s = voxel >> 6, (voxel >> 3) & 7, voxel & 7
    code = (
        (4 * octant[0] + (p >> 1)) * 64 + (4 * octant[1] + (q >> 1)) * 8 + 4 * octant[2] + (s >> 1)
    )
    spread = dot(coarse[parent], ones_where(iota((VOX, VOX), 0) == code)).astype(BF16)
    kind = 4 * (p & 1) + 2 * (q & 1) + (s & 1)
    lifted = jnp.zeros((CH, VOX), F32)
    for k in range(8):
        lifted = lifted + dot(up[k], spread * ones_where(kind == k))
    hidden = (lifted + skip[0].astype(F32)) * occupied_of(counts, slot)
    own[slot, 0:CH, :] = hidden.astype(BF16)
    own[slot, CH:ROWS, :] = meta_rows(position)
    columns = face_columns(own[slot], slot)

    @pl.when(slot == 0)
    def _():
        total[...] = columns

    @pl.when(slot == 1)
    def _():
        store_faces(faces, total[...] + columns)


def edges_kernel(faces, from_low, from_high, to_high, to_low):
    row = iota((ROWS, FACE), 0)
    lane = iota((1, FACE), 1)
    inside = lane & 15
    for target, face, edge, shift in ((to_high, 2, 56, -16.0), (to_low, 3, 0, 16.0)):
        source = (inside >> 3) * 64 + edge + (inside & 7)
        first = ones_where(iota((FACE, FACE), 0) == jnp.where(lane < 16, source, -1))
        second = ones_where(
            iota((FACE, FACE), 0) == jnp.where((lane >= 16) & (lane < 32), source, -1)
        )
        value = dot(from_low[...], first) + dot(from_high[...], second)
        value = value + jnp.where(row == CH + 1, shift, 0.0)
        target[:, 0:FACE] = faces[face]
        target[:, FACE : 2 * FACE] = value.astype(BF16)


def gather_sources(source, own, low_x, high_x, low_y, high_y):
    source[:, 0:VOX] = own[0]
    source[:, VOX : 2 * VOX] = own[1]
    start = 2 * VOX
    source[:, start : start + FACE] = low_x[...]
    source[:, start + FACE : start + 2 * FACE] = high_x[...]
    start = start + 2 * FACE
    source[:, start : start + 2 * FACE] = low_y[...]
    source[:, start + 2 * FACE : start + 4 * FACE] = high_y[...]


def fill_taps(source, frame, taps, position):
    meta = source[CH:ROWS, :].astype(F32).astype(jnp.int32)
    x = meta[0:1, :] - 8 * position[0] + 1
    y = meta[1:2, :] - 8 * position[1] + 1
    z = meta[2:3, :] - 8 * position[2] + 1
    near = (x >= 0) & (x < 10) & (y >= 0) & (y < 10) & (z >= 0) & (z < 10)
    code = jnp.where(near, x * 128 + y * 10 + z, -1)
    values = source[0:CH, :]
    for pair in range(PLANES // 2):
        place = ones_where(iota((256, SOURCES), 0) + 256 * pair == code)
        frame[:, 256 * pair : 256 * pair + 256] = dot_nt(values, place).astype(BF16)
    lane = iota((1, 9 * 128), 1)
    shift = lane >> 7
    inner = lane & 127
    step_y = jnp.where(shift >= 6, 2, jnp.where(shift >= 3, 1, 0))
    step_z = shift - 3 * step_y
    origin = (inner >> 6) * 128 + (((inner >> 3) & 7) + step_y) * 10 + (inner & 7) + step_z
    shifts = ones_where(iota((256, 9 * 128), 0) == origin)
    for pair in range(PLANES // 2):
        moved = dot(frame[:, 256 * pair : 256 * pair + 256], shifts).astype(BF16)
        for g in range(9):
            part = moved[:, 128 * g : 128 * g + 128]
            first, middle, last = (slice((9 * k + g) * CH, (9 * k + g + 1) * CH) for k in range(3))
            if pair < 4:
                taps[first, 128 * pair : 128 * pair + 128] = part
            if pair > 0:
                at = slice(128 * pair - 128, 128 * pair)
                taps[last, at] = part
                taps[middle, at] = jnp.concatenate(
                    [taps[first, at][:, 64:128], part[:, 0:64]], axis=1
                )


def forward_kernel(
    fine, counts, core, own, low_x, high_x, low_y, high_y, cot, weight,
    grad, faces, keep, send, source, frame, taps, total, sums,
):
    slot = pl.program_id(0)
    position = [fine[slot, axis] for axis in range(3)]

    @pl.when(slot == 0)
    def _():
        gather_sources(source, own, low_x, high_x, low_y, high_y)
        sums[...] = jnp.zeros_like(sums)

    fill_taps(source, frame, taps, position)
    occupied = occupied_of(counts, slot)
    for half in range(2):
        at = slice(256 * half, 256 * half + 256)
        pre = dot(weight[...], taps[:, at])
        sigma = jax.nn.sigmoid(pre)
        value = cot[0, :, at].astype(F32) * (sigma * (1.0 + pre * (1.0 - sigma))) * occupied
        grad[slot, 0:CH, at] = value.astype(BF16)
    grad[slot, CH:ROWS, :] = meta_rows(position)
    values = grad[slot, 0:CH, :]
    for start in range(0, TAPS, 512):
        size = min(512, TAPS - start)
        sums[:, start : start + size] += dot_nt(values, taps[start : start + size, :])
    columns = face_columns(grad[slot], slot)

    @pl.when(slot == 0)
    def _():
        total[...] = columns

    @pl.when(slot == 1)
    def _():
        store_faces(faces, total[...] + columns)
        part = CH // (ZH * CORES)
        mine = core[0]
        for high in range(ZH):
            own_start = pl.multiple_of((2 * high + mine) * part, 8)
            other_start = pl.multiple_of((2 * high + 1 - mine) * part, 8)
            keep[high] = sums[pl.ds(own_start, part), :]
            send[high] = sums[pl.ds(other_start, part), :].astype(BF16)


def backward_kernel(
    fine, coarse_pos, parents, counts, own, low_x, high_x, low_y, high_y, weight, up,
    skip_grad, coarse_grad, source, frame, taps,
):
    slot = pl.program_id(0)
    parent, position, octant = slot_scalars(fine, coarse_pos, parents, slot)

    @pl.when(slot == 0)
    def _():
        gather_sources(source, own, low_x, high_x, low_y, high_y)
        coarse_grad[...] = jnp.zeros_like(coarse_grad)

    fill_taps(source, frame, taps, position)
    occupied = occupied_of(counts, slot)
    for half in range(2):
        at = slice(256 * half, 256 * half + 256)
        skip_grad[0, :, at] = (dot(weight[...], taps[:, at]) * occupied).astype(BF16)
    lane = iota((1, 8 * 128), 1)
    kind = lane >> 7
    inner = lane & 127
    voxel = (
        (2 * (inner >> 4) + (kind >> 2)) * 64
        + (2 * ((inner >> 2) & 3) + ((kind >> 1) & 1)) * 8
        + 2 * (inner & 3)
        + (kind & 1)
    )
    voxel = jnp.where(inner < 64, voxel, -1)
    grouped = dot(skip_grad[0], ones_where(iota((VOX, 8 * 128), 0) == voxel)).astype(BF16)
    folded = jnp.zeros((CH, 128), F32)
    for k in range(8):
        folded = folded + dot(up[k], grouped[:, 128 * k : 128 * k + 128])
    cell = iota((1, VOX), 1)
    p, q, s = cell >> 6, (cell >> 3) & 7, cell & 7
    inside = ((p >> 2) == octant[0]) & ((q >> 2) == octant[1]) & ((s >> 2) == octant[2])
    code = jnp.where(inside, (p & 3) * 16 + (q & 3) * 4 + (s & 3), -1)
    placed = dot(folded.astype(BF16), ones_where(iota((128, VOX), 0) == code))
    coarse_grad[parent] = (coarse_grad[parent].astype(F32) + placed).astype(BF16)


def flatten_kernel(weight, flat):
    for pair in range(OFFSETS // 2):
        flat[:, 384 * pair : 384 * pair + 384] = jnp.concatenate(
            [weight[2 * pair], weight[2 * pair + 1]], axis=1
        )
    flat[:, TAPS - CH : TAPS] = weight[OFFSETS - 1]


def flatten_back_kernel(weight, up, flat, up_back):
    last = OFFSETS - 1
    for pair in range(OFFSETS // 2):
        flat[:, 384 * pair : 384 * pair + 384] = jnp.concatenate(
            [weight[last - 2 * pair].T, weight[last - 2 * pair - 1].T], axis=1
        )
    flat[:, TAPS - CH : TAPS] = weight[0].T
    for k in range(8):
        up_back[k] = up[k].T


def pack_kernel(high, own, arrived, packed):
    weights = [jnp.where(high[0] == h, 0.0, 1.0).astype(F32) for h in range(ZH)]

    def tile(index):
        at = slice(128 * index, 128 * index + 128)
        value = own[:, at]
        for h in range(ZH):
            value = value + weights[h] * arrived[h, :, at].astype(F32)
        return value

    part = own.shape[0]
    for pair in range(TILES // 2):
        both = jnp.concatenate([tile(2 * pair), tile(2 * pair + 1)], axis=0)
        packed[2 * part * pair : 2 * part * pair + 2 * part, :] = both.astype(BF16)
    start = part * (TILES - 1)
    rest = packed.shape[0] - start - part
    tail = jnp.concatenate([tile(TILES - 1), jnp.zeros((rest, 128), F32)], axis=0)
    packed[start:, :] = tail.astype(BF16)


def sum_kernel(pieces, out):
    out[...] = jnp.sum(pieces[...].astype(F32), axis=0).astype(BF16)


def total_kernel(pieces, spread):
    total = jnp.sum(pieces[...].astype(F32), axis=0, keepdims=True).astype(BF16)
    spread[...] = jnp.broadcast_to(total, spread.shape)


def unpack_kernel(packed, out):
    part = out.shape[1]

    def tiles(index):
        both = packed[2 * part * index : 2 * part * index + 2 * part, :].astype(F32)
        return both[0:part], both[part : 2 * part]

    loaded = []
    for index in range(TILES // 2):
        loaded.extend(tiles(index))
    start = part * (TILES - 1)
    loaded.append(packed[start : start + 2 * part - 8 - 8, :].astype(F32)[0:part])
    for pair in range(OFFSETS // 2):
        wide = jnp.concatenate(loaded[3 * pair : 3 * pair + 3], axis=1)
        out[2 * pair] = wide[:, 0:CH]
        out[2 * pair + 1] = wide[:, CH : 2 * CH]
    wide = jnp.concatenate(loaded[TILES - 2 : TILES], axis=1)
    out[OFFSETS - 1] = wide[:, 0:CH]


SMEM = pl.BlockSpec(memory_space=pltpu.SMEM)
WHOLE = pl.BlockSpec(memory_space=pltpu.VMEM)


def whole(*shape):
    return pl.BlockSpec(shape, lambda slot: (0,) * len(shape))


def one_slot(*shape):
    return pl.BlockSpec((1,) + shape, lambda slot: (slot,) + (0,) * len(shape))


def shaped(shape, kind=BF16):
    return jax.ShapeDtypeStruct(shape, kind)


def cost(flops, moved):
    return pl.CostEstimate(flops=flops, bytes_accessed=moved, transcendentals=0)


SOURCE_SPECS = [
    whole(2, ROWS, VOX),
    whole(ROWS, FACE),
    whole(ROWS, FACE),
    whole(ROWS, 2 * FACE),
    whole(ROWS, 2 * FACE),
]
TAP_SCRATCH = [
    pltpu.VMEM((ROWS, SOURCES), BF16),
    pltpu.VMEM((CH, 128 * PLANES), BF16),
    pltpu.VMEM((TAPS, VOX), BF16),
]


def make_hidden(fine, coarse_pos, parents, counts, skip, coarse, up):
    return pl.pallas_call(
        hidden_kernel,
        grid=(2,),
        in_specs=[SMEM] * 4
        + [one_slot(CH, VOX), whole(2, CH, VOX), whole(8, CH, CH)],
        out_specs=[whole(2, ROWS, VOX), whole(4, ROWS, FACE)],
        out_shape=[shaped((2, ROWS, VOX)), shaped((4, ROWS, FACE))],
        scratch_shapes=[pltpu.VMEM((ROWS, 4 * FACE), F32)],
        cost_estimate=cost(2_000_000_000, 3_000_000),
        interpret=INTERPRET,
        name="hidden",
    )(fine, coarse_pos, parents, counts, skip, coarse, up)


def small_kernel(body, outs, vmem=None):
    return pl.pallas_call(
        body,
        out_shape=outs,
        compiler_params=pltpu.CompilerParams(vmem_limit_bytes=vmem),
        cost_estimate=cost(1_000_000, 3_000_000),
        interpret=INTERPRET,
    )


def both_ways(axis, to_high, to_low):
    count = lax.axis_size(axis)
    forward = [(i, i + 1) for i in range(count - 1)]
    backward = [(target, source) for source, target in forward]
    return lax.ppermute(to_high, axis, forward), lax.ppermute(to_low, axis, backward)


def exchange(own, faces, beside_x=()):
    low_x, high_x = both_ways("gx", faces[0], faces[1])
    low_x, high_x, beside_x = lax.optimization_barrier((low_x, high_x, beside_x))
    to_high, to_low = small_kernel(edges_kernel, [shaped((ROWS, 2 * FACE))] * 2, SMALL)(
        faces, low_x, high_x
    )
    low_y, high_y = both_ways("gy", to_high, to_low)
    return (own, low_x, high_x, low_y, high_y), beside_x


def run_forward(fine, counts, core, sources, cot, weight):
    part = CH // (ZH * CORES)
    return pl.pallas_call(
        forward_kernel,
        grid=(2,),
        in_specs=[SMEM] * 3 + SOURCE_SPECS + [one_slot(CH, VOX), whole(CH, TAPS)],
        out_specs=[
            whole(2, ROWS, VOX),
            whole(4, ROWS, FACE),
            whole(ZH, part, PADDED),
            whole(ZH, part, PADDED),
        ],
        out_shape=[
            shaped((2, ROWS, VOX)),
            shaped((4, ROWS, FACE)),
            shaped((ZH, part, PADDED), F32),
            shaped((ZH, part, PADDED)),
        ],
        scratch_shapes=TAP_SCRATCH
        + [pltpu.VMEM((ROWS, 4 * FACE), F32), pltpu.VMEM((CH, PADDED), F32)],
        cost_estimate=cost(8_000_000_000, 8_000_000),
        interpret=INTERPRET,
        name="forward",
    )(fine, counts, core, *sources, cot, weight)


def run_backward(fine, coarse_pos, parents, counts, sources, weight, up):
    return pl.pallas_call(
        backward_kernel,
        grid=(2,),
        in_specs=[SMEM] * 4 + SOURCE_SPECS + [whole(CH, TAPS), whole(8, CH, CH)],
        out_specs=[one_slot(CH, VOX), whole(2, CH, VOX)],
        out_shape=[shaped((2, CH, VOX)), shaped((2, CH, VOX))],
        scratch_shapes=TAP_SCRATCH,
        cost_estimate=cost(6_000_000_000, 4_000_000),
        interpret=INTERPRET,
        name="backward",
    )(fine, coarse_pos, parents, counts, *sources, weight, up)


def gy_pairs(move):
    pairs = []
    for high in range(ZH):
        for core in range(CORES):
            to_high, to_core = move(high, core)
            pairs.append((high * CORES + core, to_high * CORES + to_core))
    return pairs


def pick(array, index):
    return lax.dynamic_index_in_dim(array, index, 0, keepdims=False)


def reduce_first(keep, send):
    high = lax.axis_index("gy") // CORES
    other = lax.ppermute(send, "gy", gy_pairs(lambda h, c: (h, 1 - c)))
    held = keep + other.astype(F32)
    groups = [[h * CORES + c for h in range(ZH)] for c in range(CORES)]
    arrived = lax.all_to_all(held.astype(BF16), "gy", 0, 0, axis_index_groups=groups, tiled=True)
    return pick(held, high), arrived, high.astype(jnp.int32).reshape(1)


def gx_groups():
    count = GROUP // SIDE
    rows = [[(z * SIDE + y) * XS + x for y in range(SIDE)] for z in range(ZL) for x in range(XS)]
    squares = [[(z * SIDE + y) * XS + x for z in range(ZL) for x in range(XS)] for y in range(SIDE)]
    assert len(rows) == count
    return rows, squares


def among(pieces, groups):
    return lax.all_to_all(pieces, "gx", 0, 0, axis_index_groups=groups, tiled=True)


def reduce_second(own, arrived, high):
    rows, squares = gx_groups()
    packed = pl.pallas_call(
        pack_kernel,
        in_specs=[SMEM, WHOLE, WHOLE],
        out_specs=WHOLE,
        out_shape=shaped((GROUP * 16, 128)),
        compiler_params=pltpu.CompilerParams(vmem_limit_bytes=SMALL),
        interpret=INTERPRET,
        name="pack",
    )(high, own, arrived)
    pieces = among(packed.reshape(SIDE, SIDE * 16, 128), rows)
    pieces = small_kernel(sum_kernel, shaped((SIDE * 16, 128)), SMALL)(pieces)
    pieces = among(pieces.reshape(SIDE, 16, 128), squares)
    spread = small_kernel(total_kernel, shaped((SIDE, 16, 128)), SMALL)(pieces)
    pieces = among(spread, squares).reshape(1, SIDE * 16, 128)
    pieces = among(jnp.broadcast_to(pieces, (SIDE, SIDE * 16, 128)), rows)
    part = own.shape[0]
    return small_kernel(unpack_kernel, shaped((OFFSETS, part, CH), F32), SMALL)(
        pieces.reshape(GROUP * 16, 128)
    )


def local(
    skip_feature_rows,
    coarse_features,
    cotangent,
    fine_coords,
    coarse_coords,
    parents,
    counts,
    conv_weight,
    up_weight,
):
    core = (lax.axis_index("gy") % CORES).astype(jnp.int32).reshape(1)
    by_offset = jnp.transpose(conv_weight, (1, 0, 2))
    weight_flat = small_kernel(flatten_kernel, shaped((CH, TAPS)))(by_offset)
    backs = small_kernel(
        flatten_back_kernel, [shaped((CH, TAPS)), shaped((8, CH, CH))]
    )(by_offset, up_weight)
    own, faces = make_hidden(
        fine_coords, coarse_coords, parents, counts, skip_feature_rows, coarse_features, up_weight
    )
    sources, (weight_back, up_back) = exchange(own, faces, tuple(backs))
    grad, grad_faces, keep, send = run_forward(
        fine_coords, counts, core, sources, cotangent, weight_flat
    )
    terms = reduce_first(keep, send)
    grad_sources, _ = exchange(grad, grad_faces)
    grad_skip, grad_coarse = run_backward(
        fine_coords, coarse_coords, parents, counts, grad_sources, weight_back, up_back
    )
    terms, grad_skip = lax.optimization_barrier((terms, grad_skip))
    grad_conv = reduce_second(*terms)
    return (grad_skip, grad_coarse, jnp.transpose(grad_conv, (1, 0, 2)))


def solution(mesh):
    in_specs = (
        P(("gx", "gy"), None, None),
        P(("gx", "gy"), None, None),
        P(("gx", "gy"), None, None),
        P(("gx", "gy"), None),
        P(("gx", "gy"), None),
        P(("gx", "gy")),
        P(("gx", "gy")),
        P(),
        P(),
    )
    out_specs = (P(("gx", "gy"), None, None), P(("gx", "gy"), None, None), P("gy", None, None))
    return jax.shard_map(local, mesh=mesh, in_specs=in_specs, out_specs=out_specs, check_vma=False)
```

```python
import functools

import jax
import jax.numpy as jnp
from jax import lax
from jax.experimental import pallas as pl
from jax.experimental.pallas import tpu as pltpu
from jax.sharding import PartitionSpec as P


CH = 192
META = 16
ROWS = CH + META
VOX = 512
OFFSETS = 27
TAPS = OFFSETS * CH
TILES = 41
PADDED = 128 * TILES
FACE = 128
SOURCES = 2 * VOX + 2 * FACE + 2 * 2 * FACE
PLANES = 10
ZH, CORES = 4, 2
GROUP = 64
SMALL = 24 * 1024 * 1024
INTERPRET = False

F32 = jnp.float32
BF16 = jnp.bfloat16


def iota(shape, dim):
    return lax.broadcasted_iota(jnp.int32, shape, dim)


def ones_where(condition):
    return jnp.where(condition, 1.0, 0.0).astype(BF16)


def dot(left, right):
    return jnp.dot(left, right, preferred_element_type=F32)


def dot_nt(left, right):
    return lax.dot_general(left, right, (((1,), (1,)), ((), ())), preferred_element_type=F32)


def slot_scalars(fine, coarse, parents, slot):
    parent = parents[slot]
    position = [fine[slot, axis] for axis in range(3)]
    octant = [fine[slot, axis] - 2 * coarse[parent, axis] for axis in range(3)]
    return parent, position, octant


def occupied_of(counts, slot):
    return jnp.where(slot < counts[0], 1.0, 0.0).astype(F32)


def meta_rows(position):
    voxel = iota((META, VOX), 1)
    row = iota((META, VOX), 0)
    x = 8 * position[0] + (voxel >> 6)
    y = 8 * position[1] + ((voxel >> 3) & 7)
    z = 8 * position[2] + (voxel & 7)
    value = jnp.where(row == 0, x, jnp.where(row == 1, y, jnp.where(row == 2, z, 0)))
    return value.astype(F32).astype(BF16)


def face_columns(block, slot):
    lane = iota((1, 4 * FACE), 1)
    face = lane >> 7
    inner = lane & 63
    x_high = 448 + inner
    y_low = (inner >> 3) * 64 + (inner & 7)
    source = jnp.where(
        face == 0, x_high, jnp.where(face == 1, inner, jnp.where(face == 2, y_low + 56, y_low))
    )
    source = jnp.where(((lane >> 6) & 1) == slot, source, -1)
    return dot(block, ones_where(iota((VOX, 4 * FACE), 0) == source))


def store_faces(faces_ref, total):
    row = iota((ROWS, FACE), 0)
    shifts = ((CH, -16.0), (CH, 16.0), (CH + 1, -16.0), (CH + 1, 16.0))
    for face, (where, shift) in enumerate(shifts):
        part = total[:, face * FACE : (face + 1) * FACE]
        faces_ref[face] = (part + jnp.where(row == where, shift, 0.0)).astype(BF16)


def hidden_kernel(fine, coarse_pos, parents, counts, skip, coarse, up, own, faces, total):
    slot = pl.program_id(0)
    parent, position, octant = slot_scalars(fine, coarse_pos, parents, slot)
    voxel = iota((1, VOX), 1)
    p, q, s = voxel >> 6, (voxel >> 3) & 7, voxel & 7
    code = (
        (4 * octant[0] + (p >> 1)) * 64 + (4 * octant[1] + (q >> 1)) * 8 + 4 * octant[2] + (s >> 1)
    )
    spread = dot(coarse[parent], ones_where(iota((VOX, VOX), 0) == code)).astype(BF16)
    kind = 4 * (p & 1) + 2 * (q & 1) + (s & 1)
    lifted = jnp.zeros((CH, VOX), F32)
    for k in range(8):
        lifted = lifted + dot(up[k], spread * ones_where(kind == k))
    hidden = (lifted + skip[0].astype(F32)) * occupied_of(counts, slot)
    own[slot, 0:CH, :] = hidden.astype(BF16)
    own[slot, CH:ROWS, :] = meta_rows(position)
    columns = face_columns(own[slot], slot)

    @pl.when(slot == 0)
    def _():
        total[...] = columns

    @pl.when(slot == 1)
    def _():
        store_faces(faces, total[...] + columns)


def edges_kernel(faces, from_low, from_high, to_high, to_low):
    row = iota((ROWS, FACE), 0)
    lane = iota((1, FACE), 1)
    inside = lane & 15
    for target, face, edge, shift in ((to_high, 2, 56, -16.0), (to_low, 3, 0, 16.0)):
        source = (inside >> 3) * 64 + edge + (inside & 7)
        first = ones_where(iota((FACE, FACE), 0) == jnp.where(lane < 16, source, -1))
        second = ones_where(
            iota((FACE, FACE), 0) == jnp.where((lane >= 16) & (lane < 32), source, -1)
        )
        value = dot(from_low[...], first) + dot(from_high[...], second)
        value = value + jnp.where(row == CH + 1, shift, 0.0)
        target[:, 0:FACE] = faces[face]
        target[:, FACE : 2 * FACE] = value.astype(BF16)


def gather_sources(source, own, low_x, high_x, low_y, high_y):
    source[:, 0:VOX] = own[0]
    source[:, VOX : 2 * VOX] = own[1]
    start = 2 * VOX
    source[:, start : start + FACE] = low_x[...]
    source[:, start + FACE : start + 2 * FACE] = high_x[...]
    start = start + 2 * FACE
    source[:, start : start + 2 * FACE] = low_y[...]
    source[:, start + 2 * FACE : start + 4 * FACE] = high_y[...]


def fill_taps(source, frame, taps, position):
    meta = source[CH:ROWS, :].astype(F32).astype(jnp.int32)
    x = meta[0:1, :] - 8 * position[0] + 1
    y = meta[1:2, :] - 8 * position[1] + 1
    z = meta[2:3, :] - 8 * position[2] + 1
    near = (x >= 0) & (x < 10) & (y >= 0) & (y < 10) & (z >= 0) & (z < 10)
    code = jnp.where(near, x * 128 + y * 10 + z, -1)
    values = source[0:CH, :]
    for pair in range(PLANES // 2):
        place = ones_where(iota((256, SOURCES), 0) + 256 * pair == code)
        frame[:, 256 * pair : 256 * pair + 256] = dot_nt(values, place).astype(BF16)
    lane = iota((1, 9 * 128), 1)
    shift = lane >> 7
    inner = lane & 127
    step_y = jnp.where(shift >= 6, 2, jnp.where(shift >= 3, 1, 0))
    step_z = shift - 3 * step_y
    origin = (inner >> 6) * 128 + (((inner >> 3) & 7) + step_y) * 10 + (inner & 7) + step_z
    shifts = ones_where(iota((256, 9 * 128), 0) == origin)
    for pair in range(PLANES // 2):
        moved = dot(frame[:, 256 * pair : 256 * pair + 256], shifts).astype(BF16)
        for g in range(9):
            part = moved[:, 128 * g : 128 * g + 128]
            first, middle, last = (slice((9 * k + g) * CH, (9 * k + g + 1) * CH) for k in range(3))
            if pair < 4:
                taps[first, 128 * pair : 128 * pair + 128] = part
            if pair > 0:
                at = slice(128 * pair - 128, 128 * pair)
                taps[last, at] = part
                taps[middle, at] = jnp.concatenate(
                    [taps[first, at][:, 64:128], part[:, 0:64]], axis=1
                )


def forward_kernel(
    fine, counts, core, own, low_x, high_x, low_y, high_y, cot, weight,
    grad, faces, keep, send, source, frame, taps, total, sums,
):
    slot = pl.program_id(0)
    position = [fine[slot, axis] for axis in range(3)]

    @pl.when(slot == 0)
    def _():
        gather_sources(source, own, low_x, high_x, low_y, high_y)
        sums[...] = jnp.zeros_like(sums)

    fill_taps(source, frame, taps, position)
    occupied = occupied_of(counts, slot)
    for half in range(2):
        at = slice(256 * half, 256 * half + 256)
        pre = dot(weight[...], taps[:, at])
        sigma = jax.nn.sigmoid(pre)
        value = cot[0, :, at].astype(F32) * (sigma * (1.0 + pre * (1.0 - sigma))) * occupied
        grad[slot, 0:CH, at] = value.astype(BF16)
    grad[slot, CH:ROWS, :] = meta_rows(position)
    values = grad[slot, 0:CH, :]
    for start in range(0, TAPS, 512):
        size = min(512, TAPS - start)
        sums[:, start : start + size] += dot_nt(values, taps[start : start + size, :])
    columns = face_columns(grad[slot], slot)

    @pl.when(slot == 0)
    def _():
        total[...] = columns

    @pl.when(slot == 1)
    def _():
        store_faces(faces, total[...] + columns)
        part = CH // (ZH * CORES)
        mine = core[0]
        for high in range(ZH):
            own_start = pl.multiple_of((2 * high + mine) * part, 8)
            other_start = pl.multiple_of((2 * high + 1 - mine) * part, 8)
            keep[high] = sums[pl.ds(own_start, part), :]
            send[high] = sums[pl.ds(other_start, part), :].astype(BF16)


def backward_kernel(slot, fine, coarse_pos, parents, counts, own, *refs):
    low_x, high_x, low_y, high_y, weight, up = refs[:6]
    skip_grad, coarse_grad, source, frame, taps = refs[-5:]
    parent, position, octant = slot_scalars(fine, coarse_pos, parents, slot)

    gather_sources(source, own, low_x, high_x, low_y, high_y)
    coarse_grad[...] = jnp.zeros_like(coarse_grad) if slot == 0 else refs[7][...]

    fill_taps(source, frame, taps, position)
    occupied = occupied_of(counts, slot)
    for half in range(2):
        at = slice(256 * half, 256 * half + 256)
        skip_grad[0, :, at] = (dot(weight[...], taps[:, at]) * occupied).astype(BF16)
    lane = iota((1, 8 * 128), 1)
    kind = lane >> 7
    inner = lane & 127
    voxel = (
        (2 * (inner >> 4) + (kind >> 2)) * 64
        + (2 * ((inner >> 2) & 3) + ((kind >> 1) & 1)) * 8
        + 2 * (inner & 3)
        + (kind & 1)
    )
    voxel = jnp.where(inner < 64, voxel, -1)
    grouped = dot(skip_grad[0], ones_where(iota((VOX, 8 * 128), 0) == voxel)).astype(BF16)
    folded = jnp.zeros((CH, 128), F32)
    for k in range(8):
        folded = folded + dot(up[k], grouped[:, 128 * k : 128 * k + 128])
    cell = iota((1, VOX), 1)
    p, q, s = cell >> 6, (cell >> 3) & 7, cell & 7
    inside = ((p >> 2) == octant[0]) & ((q >> 2) == octant[1]) & ((s >> 2) == octant[2])
    code = jnp.where(inside, (p & 3) * 16 + (q & 3) * 4 + (s & 3), -1)
    placed = dot(folded.astype(BF16), ones_where(iota((128, VOX), 0) == code))
    coarse_grad[parent] = (coarse_grad[parent].astype(F32) + placed).astype(BF16)


def flatten_kernel(weight, flat):
    for pair in range(OFFSETS // 2):
        flat[:, 384 * pair : 384 * pair + 384] = jnp.concatenate(
            [weight[2 * pair], weight[2 * pair + 1]], axis=1
        )
    flat[:, TAPS - CH : TAPS] = weight[OFFSETS - 1]


def flatten_back_kernel(weight, up, flat, up_back):
    last = OFFSETS - 1
    for pair in range(OFFSETS // 2):
        flat[:, 384 * pair : 384 * pair + 384] = jnp.concatenate(
            [weight[last - 2 * pair].T, weight[last - 2 * pair - 1].T], axis=1
        )
    flat[:, TAPS - CH : TAPS] = weight[0].T
    for k in range(8):
        up_back[k] = up[k].T


def pack_kernel(own, first, second, third, packed):
    def tile(index):
        at = slice(128 * index, 128 * index + 128)
        value = own[:, at]
        for piece in (first, second, third):
            value = value + piece[:, at].astype(F32)
        return value

    part = own.shape[0]
    for pair in range(TILES // 2):
        both = jnp.concatenate([tile(2 * pair), tile(2 * pair + 1)], axis=0)
        packed[2 * part * pair : 2 * part * pair + 2 * part, :] = both.astype(BF16)
    start = part * (TILES - 1)
    rest = packed.shape[0] - start - part
    tail = jnp.concatenate([tile(TILES - 1), jnp.zeros((rest, 128), F32)], axis=0)
    packed[start:, :] = tail.astype(BF16)


def total_kernel(pieces, spread):
    total = jnp.sum(pieces[...].astype(F32), axis=0, keepdims=True).astype(BF16)
    spread[...] = jnp.broadcast_to(total, spread.shape)


def unpack_kernel(packed, out):
    part = out.shape[1]

    def tiles(index):
        both = packed[2 * part * index : 2 * part * index + 2 * part, :].astype(F32)
        return both[0:part], both[part : 2 * part]

    loaded = []
    for index in range(TILES // 2):
        loaded.extend(tiles(index))
    start = part * (TILES - 1)
    loaded.append(packed[start : start + 2 * part - 8 - 8, :].astype(F32)[0:part])
    for pair in range(OFFSETS // 2):
        wide = jnp.concatenate(loaded[3 * pair : 3 * pair + 3], axis=1)
        out[2 * pair] = wide[:, 0:CH]
        out[2 * pair + 1] = wide[:, CH : 2 * CH]
    wide = jnp.concatenate(loaded[TILES - 2 : TILES], axis=1)
    out[OFFSETS - 1] = wide[:, 0:CH]


SMEM = pl.BlockSpec(memory_space=pltpu.SMEM)


def whole(*shape):
    return pl.BlockSpec(shape, lambda slot: (0,) * len(shape))


def one_slot(*shape):
    return pl.BlockSpec((1,) + shape, lambda slot: (slot,) + (0,) * len(shape))


def shaped(shape, kind=BF16):
    return jax.ShapeDtypeStruct(shape, kind)


def cost(flops, moved):
    return pl.CostEstimate(flops=flops, bytes_accessed=moved, transcendentals=0)


SOURCE_SPECS = [
    whole(2, ROWS, VOX),
    whole(ROWS, FACE),
    whole(ROWS, FACE),
    whole(ROWS, 2 * FACE),
    whole(ROWS, 2 * FACE),
]
TAP_SCRATCH = [
    pltpu.VMEM((ROWS, SOURCES), BF16),
    pltpu.VMEM((CH, 128 * PLANES), BF16),
    pltpu.VMEM((TAPS, VOX), BF16),
]


def make_hidden(fine, coarse_pos, parents, counts, skip, coarse, up):
    return pl.pallas_call(
        hidden_kernel,
        grid=(2,),
        in_specs=[SMEM] * 4
        + [one_slot(CH, VOX), whole(2, CH, VOX), whole(8, CH, CH)],
        out_specs=[whole(2, ROWS, VOX), whole(4, ROWS, FACE)],
        out_shape=[shaped((2, ROWS, VOX)), shaped((4, ROWS, FACE))],
        scratch_shapes=[pltpu.VMEM((ROWS, 4 * FACE), F32)],
        cost_estimate=cost(2_000_000_000, 3_000_000),
        interpret=INTERPRET,
        name="hidden",
    )(fine, coarse_pos, parents, counts, skip, coarse, up)


def small_kernel(body, outs, vmem=None):
    return pl.pallas_call(
        body,
        out_shape=outs,
        compiler_params=pltpu.CompilerParams(vmem_limit_bytes=vmem),
        cost_estimate=cost(1_000_000, 3_000_000),
        interpret=INTERPRET,
    )


def both_ways(axis, to_high, to_low):
    count = lax.axis_size(axis)
    forward = [(i, i + 1) for i in range(count - 1)]
    backward = [(target, source) for source, target in forward]
    return lax.ppermute(to_high, axis, forward), lax.ppermute(to_low, axis, backward)


def exchange(own, faces, beside_x=()):
    low_x, high_x = both_ways("gx", faces[0], faces[1])
    low_x, high_x, beside_x = lax.optimization_barrier((low_x, high_x, beside_x))
    to_high, to_low = small_kernel(edges_kernel, [shaped((ROWS, 2 * FACE))] * 2, SMALL)(
        faces, low_x, high_x
    )
    low_y, high_y = both_ways("gy", to_high, to_low)
    return (own, low_x, high_x, low_y, high_y), beside_x


def run_forward(fine, counts, core, sources, cot, weight):
    part = CH // (ZH * CORES)
    return pl.pallas_call(
        forward_kernel,
        grid=(2,),
        in_specs=[SMEM] * 3 + SOURCE_SPECS + [one_slot(CH, VOX), whole(CH, TAPS)],
        out_specs=[
            whole(2, ROWS, VOX),
            whole(4, ROWS, FACE),
            whole(ZH, part, PADDED),
            whole(ZH, part, PADDED),
        ],
        out_shape=[
            shaped((2, ROWS, VOX)),
            shaped((4, ROWS, FACE)),
            shaped((ZH, part, PADDED), F32),
            shaped((ZH, part, PADDED)),
        ],
        scratch_shapes=TAP_SCRATCH
        + [pltpu.VMEM((ROWS, 4 * FACE), F32), pltpu.VMEM((CH, PADDED), F32)],
        cost_estimate=cost(8_000_000_000, 8_000_000),
        interpret=INTERPRET,
        name="forward",
    )(fine, counts, core, *sources, cot, weight)


def run_backward(slot, fine, coarse_pos, parents, counts, sources, weight, up, before=()):
    aliases = {11: 0} if before else {}
    earlier = [pl.BlockSpec(memory_space=pl.ANY), whole(2, CH, VOX)] if before else []
    return pl.pallas_call(
        functools.partial(backward_kernel, slot),
        grid=(1,),
        in_specs=[SMEM] * 4 + SOURCE_SPECS + [whole(CH, TAPS), whole(8, CH, CH)] + earlier,
        out_specs=[
            pl.BlockSpec((1, CH, VOX), lambda step: (slot, 0, 0)),
            whole(2, CH, VOX),
        ],
        out_shape=[shaped((2, CH, VOX)), shaped((2, CH, VOX))],
        scratch_shapes=TAP_SCRATCH,
        input_output_aliases=aliases,
        cost_estimate=cost(3_000_000_000, 4_000_000),
        interpret=INTERPRET,
    )(fine, coarse_pos, parents, counts, *sources, weight, up, *before)


def gy_pairs(move):
    pairs = []
    for high in range(ZH):
        for core in range(CORES):
            to_high, to_core = move(high, core)
            pairs.append((high * CORES + core, to_high * CORES + to_core))
    return pairs


def pick(array, index):
    return lax.dynamic_index_in_dim(array, index, 0, keepdims=False)


def reduce_first(keep, send):
    high = lax.axis_index("gy") // CORES
    other = lax.ppermute(send, "gy", gy_pairs(lambda h, c: (h, 1 - c)))
    held = keep + other.astype(F32)
    arrived = []
    for step in (1, 3, 2):
        piece = pick(held, (high + step) % ZH).astype(BF16)
        arrived.append(lax.ppermute(piece, "gy", gy_pairs(lambda h, c, s=step: ((h + s) % ZH, c))))
    return (pick(held, high), *arrived)


def reduce_second(terms):
    packed = small_kernel(pack_kernel, shaped((GROUP * 16, 128)), SMALL)(*terms)
    pieces = lax.all_to_all(packed.reshape(GROUP, 16, 128), "gx", 0, 0, tiled=True)
    spread = small_kernel(total_kernel, shaped((GROUP, 16, 128)), SMALL)(pieces)
    packed = lax.all_to_all(spread, "gx", 0, 0, tiled=True)
    packed = packed.reshape(GROUP * 16, 128)
    part = terms[0].shape[0]
    return small_kernel(unpack_kernel, shaped((OFFSETS, part, CH), F32), SMALL)(packed)


def local(
    skip_feature_rows,
    coarse_features,
    cotangent,
    fine_coords,
    coarse_coords,
    parents,
    counts,
    conv_weight,
    up_weight,
):
    core = (lax.axis_index("gy") % CORES).astype(jnp.int32).reshape(1)
    by_offset = jnp.transpose(conv_weight, (1, 0, 2))
    weight_flat = small_kernel(flatten_kernel, shaped((CH, TAPS)))(by_offset)
    backs = small_kernel(
        flatten_back_kernel, [shaped((CH, TAPS)), shaped((8, CH, CH))]
    )(by_offset, up_weight)
    own, faces = make_hidden(
        fine_coords, coarse_coords, parents, counts, skip_feature_rows, coarse_features, up_weight
    )
    sources, (weight_back, up_back) = exchange(own, faces, tuple(backs))
    grad, grad_faces, keep, send = run_forward(
        fine_coords, counts, core, sources, cotangent, weight_flat
    )
    terms = reduce_first(keep, send)
    grad_sources, _ = exchange(grad, grad_faces)
    scalars = (fine_coords, coarse_coords, parents, counts)
    weights = (weight_back, up_back)
    first = run_backward(0, *scalars, grad_sources, *weights)
    grad_skip, grad_coarse = run_backward(1, *scalars, grad_sources, *weights, tuple(first))
    grad_conv = reduce_second(terms)
    return (grad_skip, grad_coarse, jnp.transpose(grad_conv, (1, 0, 2)))


def solution(mesh):
    in_specs = (
        P(("gx", "gy"), None, None),
        P(("gx", "gy"), None, None),
        P(("gx", "gy"), None, None),
        P(("gx", "gy"), None),
        P(("gx", "gy"), None),
        P(("gx", "gy")),
        P(("gx", "gy")),
        P(),
        P(),
    )
    out_specs = (P(("gx", "gy"), None, None), P(("gx", "gy"), None, None), P("gy", None, None))
    return jax.shard_map(local, mesh=mesh, in_specs=in_specs, out_specs=out_specs, check_vma=False)
```

```python
import functools

import jax
import jax.numpy as jnp
from jax import lax
from jax.experimental import pallas as pl
from jax.experimental.pallas import tpu as pltpu
from jax.sharding import PartitionSpec as P


CH = 192
META = 16
ROWS = CH + META
VOX = 512
OFFSETS = 27
TAPS = OFFSETS * CH
TILES = 41
PADDED = 128 * TILES
FACE = 128
SOURCES = 2 * VOX + 2 * FACE + 2 * 2 * FACE
PLANES = 10
ZH, CORES = 4, 2
GROUP = 64
SMALL = 24 * 1024 * 1024
INTERPRET = False

F32 = jnp.float32
BF16 = jnp.bfloat16


def iota(shape, dim):
    return lax.broadcasted_iota(jnp.int32, shape, dim)


def ones_where(condition):
    return jnp.where(condition, 1.0, 0.0).astype(BF16)


def dot(left, right):
    return jnp.dot(left, right, preferred_element_type=F32)


def dot_nt(left, right):
    return lax.dot_general(left, right, (((1,), (1,)), ((), ())), preferred_element_type=F32)


def slot_scalars(fine, coarse, parents, slot):
    parent = parents[slot]
    position = [fine[slot, axis] for axis in range(3)]
    octant = [fine[slot, axis] - 2 * coarse[parent, axis] for axis in range(3)]
    return parent, position, octant


def occupied_of(counts, slot):
    return jnp.where(slot < counts[0], 1.0, 0.0).astype(F32)


def meta_rows(position):
    voxel = iota((META, VOX), 1)
    row = iota((META, VOX), 0)
    x = 8 * position[0] + (voxel >> 6)
    y = 8 * position[1] + ((voxel >> 3) & 7)
    z = 8 * position[2] + (voxel & 7)
    value = jnp.where(row == 0, x, jnp.where(row == 1, y, jnp.where(row == 2, z, 0)))
    return value.astype(F32).astype(BF16)


def face_columns(block, slot):
    lane = iota((1, 4 * FACE), 1)
    face = lane >> 7
    inner = lane & 63
    x_high = 448 + inner
    y_low = (inner >> 3) * 64 + (inner & 7)
    source = jnp.where(
        face == 0, x_high, jnp.where(face == 1, inner, jnp.where(face == 2, y_low + 56, y_low))
    )
    source = jnp.where(((lane >> 6) & 1) == slot, source, -1)
    return dot(block, ones_where(iota((VOX, 4 * FACE), 0) == source))


def store_faces(faces, total):
    row = iota((ROWS, FACE), 0)
    shifts = ((CH, -16.0), (CH, 16.0), (CH + 1, -16.0), (CH + 1, 16.0))
    for face, (where, shift) in enumerate(shifts):
        part = total[:, face * FACE : (face + 1) * FACE]
        faces[face][...] = (part + jnp.where(row == where, shift, 0.0)).astype(BF16)


def hidden_kernel(fine, coarse_pos, parents, counts, skip, coarse, up, own, *refs):
    faces, total = refs[:4], refs[4]
    slot = pl.program_id(0)
    parent, position, octant = slot_scalars(fine, coarse_pos, parents, slot)
    voxel = iota((1, VOX), 1)
    p, q, s = voxel >> 6, (voxel >> 3) & 7, voxel & 7
    code = (
        (4 * octant[0] + (p >> 1)) * 64 + (4 * octant[1] + (q >> 1)) * 8 + 4 * octant[2] + (s >> 1)
    )
    spread = dot(coarse[parent], ones_where(iota((VOX, VOX), 0) == code)).astype(BF16)
    kind = 4 * (p & 1) + 2 * (q & 1) + (s & 1)
    lifted = jnp.zeros((CH, VOX), F32)
    for k in range(8):
        lifted = lifted + dot(up[k], spread * ones_where(kind == k))
    hidden = (lifted + skip[0].astype(F32)) * occupied_of(counts, slot)
    own[slot, 0:CH, :] = hidden.astype(BF16)
    own[slot, CH:ROWS, :] = meta_rows(position)
    columns = face_columns(own[slot], slot)

    @pl.when(slot == 0)
    def _():
        total[...] = columns

    @pl.when(slot == 1)
    def _():
        store_faces(faces, total[...] + columns)


def edges_kernel(y_high, y_low, from_low, from_high, to_high, to_low):
    row = iota((ROWS, FACE), 0)
    lane = iota((1, FACE), 1)
    inside = lane & 15
    for target, face, edge, shift in ((to_high, y_high, 56, -16.0), (to_low, y_low, 0, 16.0)):
        source = (inside >> 3) * 64 + edge + (inside & 7)
        first = ones_where(iota((FACE, FACE), 0) == jnp.where(lane < 16, source, -1))
        second = ones_where(
            iota((FACE, FACE), 0) == jnp.where((lane >= 16) & (lane < 32), source, -1)
        )
        value = dot(from_low[...], first) + dot(from_high[...], second)
        value = value + jnp.where(row == CH + 1, shift, 0.0)
        target[:, 0:FACE] = face[...]
        target[:, FACE : 2 * FACE] = value.astype(BF16)


def gather_sources(source, own, low_x, high_x, low_y, high_y):
    source[:, 0:VOX] = own[0]
    source[:, VOX : 2 * VOX] = own[1]
    start = 2 * VOX
    source[:, start : start + FACE] = low_x[...]
    source[:, start + FACE : start + 2 * FACE] = high_x[...]
    start = start + 2 * FACE
    source[:, start : start + 2 * FACE] = low_y[...]
    source[:, start + 2 * FACE : start + 4 * FACE] = high_y[...]


def fill_taps(source, frame, taps, position):
    meta = source[CH:ROWS, :].astype(F32).astype(jnp.int32)
    x = meta[0:1, :] - 8 * position[0] + 1
    y = meta[1:2, :] - 8 * position[1] + 1
    z = meta[2:3, :] - 8 * position[2] + 1
    near = (x >= 0) & (x < 10) & (y >= 0) & (y < 10) & (z >= 0) & (z < 10)
    code = jnp.where(near, x * 128 + y * 10 + z, -1)
    values = source[0:CH, :]
    for pair in range(PLANES // 2):
        place = ones_where(iota((256, SOURCES), 0) + 256 * pair == code)
        frame[:, 256 * pair : 256 * pair + 256] = dot_nt(values, place).astype(BF16)
    lane = iota((1, 9 * 128), 1)
    shift = lane >> 7
    inner = lane & 127
    step_y = jnp.where(shift >= 6, 2, jnp.where(shift >= 3, 1, 0))
    step_z = shift - 3 * step_y
    origin = (inner >> 6) * 128 + (((inner >> 3) & 7) + step_y) * 10 + (inner & 7) + step_z
    shifts = ones_where(iota((256, 9 * 128), 0) == origin)
    for pair in range(PLANES // 2):
        moved = dot(frame[:, 256 * pair : 256 * pair + 256], shifts).astype(BF16)
        for g in range(9):
            part = moved[:, 128 * g : 128 * g + 128]
            first, middle, last = (slice((9 * k + g) * CH, (9 * k + g + 1) * CH) for k in range(3))
            if pair < 4:
                taps[first, 128 * pair : 128 * pair + 128] = part
            if pair > 0:
                at = slice(128 * pair - 128, 128 * pair)
                taps[last, at] = part
                taps[middle, at] = jnp.concatenate(
                    [taps[first, at][:, 64:128], part[:, 0:64]], axis=1
                )


def forward_kernel(
    fine, counts, core, own, low_x, high_x, low_y, high_y, cot, weight,
    grad, face0, face1, face2, face3, keep, send, source, frame, taps, total, sums,
    held_weight, arrival,
):
    faces = (face0, face1, face2, face3)
    load = pltpu.make_async_copy(weight, held_weight, arrival)
    slot = pl.program_id(0)
    position = [fine[slot, axis] for axis in range(3)]

    @pl.when(slot == 0)
    def _():
        load.start()
        gather_sources(source, own, low_x, high_x, low_y, high_y)
        sums[:, PADDED - 128 :] = jnp.zeros((CH, 128), F32)

    fill_taps(source, frame, taps, position)

    @pl.when(slot == 0)
    def _():
        load.wait()

    occupied = occupied_of(counts, slot)
    for half in range(2):
        at = slice(256 * half, 256 * half + 256)
        pre = dot(held_weight[...], taps[:, at])
        sigma = jax.nn.sigmoid(pre)
        value = cot[0, :, at].astype(F32) * (sigma * (1.0 + pre * (1.0 - sigma))) * occupied
        grad[slot, 0:CH, at] = value.astype(BF16)
    grad[slot, CH:ROWS, :] = meta_rows(position)
    values = grad[slot, 0:CH, :]
    for start in range(0, TAPS, 512):
        size = min(512, TAPS - start)
        earlier = jnp.where(slot == 0, 0.0, sums[:, start : start + size])
        sums[:, start : start + size] = earlier + dot_nt(values, taps[start : start + size, :])
    columns = face_columns(grad[slot], slot)

    @pl.when(slot == 0)
    def _():
        total[...] = columns

    @pl.when(slot == 1)
    def _():
        store_faces(faces, total[...] + columns)
        part = CH // (ZH * CORES)
        mine = core[0]
        for high in range(ZH):
            own_start = pl.multiple_of((2 * high + mine) * part, 8)
            other_start = pl.multiple_of((2 * high + 1 - mine) * part, 8)
            keep[high] = sums[pl.ds(own_start, part), :]
            send[high] = sums[pl.ds(other_start, part), :].astype(BF16)


def backward_kernel(slot, fine, coarse_pos, parents, counts, own, *refs):
    low_x, high_x, low_y, high_y, weight, up = refs[:6]
    skip_grad, coarse_grad, source, frame, taps, held_weight, arrival = refs[-7:]
    load = pltpu.make_async_copy(weight, held_weight, arrival)
    load.start()
    parent, position, octant = slot_scalars(fine, coarse_pos, parents, slot)

    gather_sources(source, own, low_x, high_x, low_y, high_y)
    coarse_grad[...] = jnp.zeros_like(coarse_grad) if slot == 0 else refs[7][...]

    fill_taps(source, frame, taps, position)
    occupied = occupied_of(counts, slot)
    load.wait()
    for half in range(2):
        at = slice(256 * half, 256 * half + 256)
        skip_grad[0, :, at] = (dot(held_weight[...], taps[:, at]) * occupied).astype(BF16)
    lane = iota((1, 8 * 128), 1)
    kind = lane >> 7
    inner = lane & 127
    voxel = (
        (2 * (inner >> 4) + (kind >> 2)) * 64
        + (2 * ((inner >> 2) & 3) + ((kind >> 1) & 1)) * 8
        + 2 * (inner & 3)
        + (kind & 1)
    )
    voxel = jnp.where(inner < 64, voxel, -1)
    grouped = dot(skip_grad[0], ones_where(iota((VOX, 8 * 128), 0) == voxel)).astype(BF16)
    folded = jnp.zeros((CH, 128), F32)
    for k in range(8):
        folded = folded + dot(up[k], grouped[:, 128 * k : 128 * k + 128])
    cell = iota((1, VOX), 1)
    p, q, s = cell >> 6, (cell >> 3) & 7, cell & 7
    inside = ((p >> 2) == octant[0]) & ((q >> 2) == octant[1]) & ((s >> 2) == octant[2])
    code = jnp.where(inside, (p & 3) * 16 + (q & 3) * 4 + (s & 3), -1)
    placed = dot(folded.astype(BF16), ones_where(iota((128, VOX), 0) == code))
    coarse_grad[parent] = (coarse_grad[parent].astype(F32) + placed).astype(BF16)


def flatten_kernel(weight, flat):
    for pair in range(OFFSETS // 2):
        flat[:, 384 * pair : 384 * pair + 384] = jnp.concatenate(
            [weight[2 * pair], weight[2 * pair + 1]], axis=1
        )
    flat[:, TAPS - CH : TAPS] = weight[OFFSETS - 1]


def flatten_back_kernel(weight, up, flat, up_back):
    last = OFFSETS - 1
    for pair in range(OFFSETS // 2):
        flat[:, 384 * pair : 384 * pair + 384] = jnp.concatenate(
            [weight[last - 2 * pair].T, weight[last - 2 * pair - 1].T], axis=1
        )
    flat[:, TAPS - CH : TAPS] = weight[0].T
    for k in range(8):
        up_back[k] = up[k].T


def pack_kernel(own, first, second, third, packed):
    def tile(index):
        at = slice(128 * index, 128 * index + 128)
        value = own[:, at]
        for piece in (first, second, third):
            value = value + piece[:, at].astype(F32)
        return value

    part = own.shape[0]
    for pair in range(TILES // 2):
        both = jnp.concatenate([tile(2 * pair), tile(2 * pair + 1)], axis=0)
        packed[2 * part * pair : 2 * part * pair + 2 * part, :] = both.astype(BF16)
    start = part * (TILES - 1)
    rest = packed.shape[0] - start - part
    tail = jnp.concatenate([tile(TILES - 1), jnp.zeros((rest, 128), F32)], axis=0)
    packed[start:, :] = tail.astype(BF16)


def total_kernel(pieces, spread):
    total = jnp.sum(pieces[...].astype(F32), axis=0, keepdims=True).astype(BF16)
    spread[...] = jnp.broadcast_to(total, spread.shape)


def unpack_kernel(packed, out):
    part = out.shape[1]

    def tiles(index):
        both = packed[2 * part * index : 2 * part * index + 2 * part, :].astype(F32)
        return both[0:part], both[part : 2 * part]

    loaded = []
    for index in range(TILES // 2):
        loaded.extend(tiles(index))
    start = part * (TILES - 1)
    loaded.append(packed[start : start + 2 * part - 8 - 8, :].astype(F32)[0:part])
    for pair in range(OFFSETS // 2):
        wide = jnp.concatenate(loaded[3 * pair : 3 * pair + 3], axis=1)
        out[2 * pair] = wide[:, 0:CH]
        out[2 * pair + 1] = wide[:, CH : 2 * CH]
    wide = jnp.concatenate(loaded[TILES - 2 : TILES], axis=1)
    out[OFFSETS - 1] = wide[:, 0:CH]


SMEM = pl.BlockSpec(memory_space=pltpu.SMEM)
ANYWHERE = pl.BlockSpec(memory_space=pl.ANY)
WEIGHT_SCRATCH = [pltpu.VMEM((CH, TAPS), BF16), pltpu.SemaphoreType.DMA]


def whole(*shape):
    return pl.BlockSpec(shape, lambda slot: (0,) * len(shape))


def one_slot(*shape):
    return pl.BlockSpec((1,) + shape, lambda slot: (slot,) + (0,) * len(shape))


def shaped(shape, kind=BF16):
    return jax.ShapeDtypeStruct(shape, kind)


def cost(flops, moved):
    return pl.CostEstimate(flops=flops, bytes_accessed=moved, transcendentals=0)


SOURCE_SPECS = [
    whole(2, ROWS, VOX),
    whole(ROWS, FACE),
    whole(ROWS, FACE),
    whole(ROWS, 2 * FACE),
    whole(ROWS, 2 * FACE),
]
TAP_SCRATCH = [
    pltpu.VMEM((ROWS, SOURCES), BF16),
    pltpu.VMEM((CH, 128 * PLANES), BF16),
    pltpu.VMEM((TAPS, VOX), BF16),
]


def make_hidden(fine, coarse_pos, parents, counts, skip, coarse, up):
    return pl.pallas_call(
        hidden_kernel,
        grid=(2,),
        in_specs=[SMEM] * 4
        + [one_slot(CH, VOX), whole(2, CH, VOX), whole(8, CH, CH)],
        out_specs=[whole(2, ROWS, VOX)] + [whole(ROWS, FACE)] * 4,
        out_shape=[shaped((2, ROWS, VOX))] + [shaped((ROWS, FACE))] * 4,
        scratch_shapes=[pltpu.VMEM((ROWS, 4 * FACE), F32)],
        cost_estimate=cost(2_000_000_000, 3_000_000),
        interpret=INTERPRET,
        name="hidden",
    )(fine, coarse_pos, parents, counts, skip, coarse, up)


def small_kernel(body, outs, vmem=None):
    return pl.pallas_call(
        body,
        out_shape=outs,
        compiler_params=pltpu.CompilerParams(vmem_limit_bytes=vmem),
        cost_estimate=cost(1_000_000, 3_000_000),
        interpret=INTERPRET,
    )


def both_ways(axis, to_high, to_low):
    count = lax.axis_size(axis)
    forward = [(i, i + 1) for i in range(count - 1)]
    backward = [(target, source) for source, target in forward]
    return lax.ppermute(to_high, axis, forward), lax.ppermute(to_low, axis, backward)


def exchange(own, faces, beside_x=()):
    low_x, high_x = both_ways("gx", faces[0], faces[1])
    low_x, high_x, beside_x = lax.optimization_barrier((low_x, high_x, beside_x))
    to_high, to_low = small_kernel(edges_kernel, [shaped((ROWS, 2 * FACE))] * 2, SMALL)(
        faces[2], faces[3], low_x, high_x
    )
    low_y, high_y = both_ways("gy", to_high, to_low)
    return (own, low_x, high_x, low_y, high_y), beside_x


def run_forward(fine, counts, core, sources, cot, weight):
    part = CH // (ZH * CORES)
    return pl.pallas_call(
        forward_kernel,
        grid=(2,),
        in_specs=[SMEM] * 3 + SOURCE_SPECS + [one_slot(CH, VOX), ANYWHERE],
        out_specs=[
            whole(2, ROWS, VOX),
            *[whole(ROWS, FACE)] * 4,
            whole(ZH, part, PADDED),
            whole(ZH, part, PADDED),
        ],
        out_shape=[
            shaped((2, ROWS, VOX)),
            *[shaped((ROWS, FACE))] * 4,
            shaped((ZH, part, PADDED), F32),
            shaped((ZH, part, PADDED)),
        ],
        scratch_shapes=TAP_SCRATCH
        + [pltpu.VMEM((ROWS, 4 * FACE), F32), pltpu.VMEM((CH, PADDED), F32)]
        + WEIGHT_SCRATCH,
        cost_estimate=cost(8_000_000_000, 8_000_000),
        interpret=INTERPRET,
        name="forward",
    )(fine, counts, core, *sources, cot, weight)


def run_backward(slot, fine, coarse_pos, parents, counts, sources, weight, up, before=()):
    aliases = {11: 0} if before else {}
    earlier = [ANYWHERE, whole(2, CH, VOX)] if before else []
    return pl.pallas_call(
        functools.partial(backward_kernel, slot),
        grid=(1,),
        in_specs=[SMEM] * 4 + SOURCE_SPECS + [ANYWHERE, whole(8, CH, CH)] + earlier,
        out_specs=[
            pl.BlockSpec((1, CH, VOX), lambda step: (slot, 0, 0)),
            whole(2, CH, VOX),
        ],
        out_shape=[shaped((2, CH, VOX)), shaped((2, CH, VOX))],
        scratch_shapes=TAP_SCRATCH + WEIGHT_SCRATCH,
        input_output_aliases=aliases,
        cost_estimate=cost(3_000_000_000, 4_000_000),
        interpret=INTERPRET,
    )(fine, coarse_pos, parents, counts, *sources, weight, up, *before)


def gy_pairs(move):
    pairs = []
    for high in range(ZH):
        for core in range(CORES):
            to_high, to_core = move(high, core)
            pairs.append((high * CORES + core, to_high * CORES + to_core))
    return pairs


def pick(array, index):
    return lax.dynamic_index_in_dim(array, index, 0, keepdims=False)


def reduce_first(keep, send):
    high = lax.axis_index("gy") // CORES
    other = lax.ppermute(send, "gy", gy_pairs(lambda h, c: (h, 1 - c)))
    held = keep + other.astype(F32)
    arrived = []
    for step in (1, 3, 2):
        piece = pick(held, (high + step) % ZH).astype(BF16)
        arrived.append(lax.ppermute(piece, "gy", gy_pairs(lambda h, c, s=step: ((h + s) % ZH, c))))
    return (pick(held, high), *arrived)


def reduce_second(terms):
    packed = small_kernel(pack_kernel, shaped((GROUP * 16, 128)), SMALL)(*terms)
    pieces = lax.all_to_all(packed.reshape(GROUP, 16, 128), "gx", 0, 0, tiled=True)
    spread = small_kernel(total_kernel, shaped((GROUP, 16, 128)), SMALL)(pieces)
    packed = lax.all_to_all(spread, "gx", 0, 0, tiled=True)
    packed = packed.reshape(GROUP * 16, 128)
    part = terms[0].shape[0]
    return small_kernel(unpack_kernel, shaped((OFFSETS, part, CH), F32), SMALL)(packed)


def local(
    skip_feature_rows,
    coarse_features,
    cotangent,
    fine_coords,
    coarse_coords,
    parents,
    counts,
    conv_weight,
    up_weight,
):
    core = (lax.axis_index("gy") % CORES).astype(jnp.int32).reshape(1)
    by_offset = jnp.transpose(conv_weight, (1, 0, 2))
    weight_flat = small_kernel(flatten_kernel, shaped((CH, TAPS)))(by_offset)
    backs = small_kernel(
        flatten_back_kernel, [shaped((CH, TAPS)), shaped((8, CH, CH))]
    )(by_offset, up_weight)
    own, *faces = make_hidden(
        fine_coords, coarse_coords, parents, counts, skip_feature_rows, coarse_features, up_weight
    )
    sources, (weight_back, up_back) = exchange(own, faces, tuple(backs))
    grad, *grad_faces, keep, send = run_forward(
        fine_coords, counts, core, sources, cotangent, weight_flat
    )
    terms = reduce_first(keep, send)
    grad_sources, _ = exchange(grad, grad_faces)
    scalars = (fine_coords, coarse_coords, parents, counts)
    weights = (weight_back, up_back)
    first = run_backward(0, *scalars, grad_sources, *weights)
    grad_skip, grad_coarse = run_backward(1, *scalars, grad_sources, *weights, tuple(first))
    grad_conv = reduce_second(terms)
    return (grad_skip, grad_coarse, jnp.transpose(grad_conv, (1, 0, 2)))


def solution(mesh):
    in_specs = (
        P(("gx", "gy"), None, None),
        P(("gx", "gy"), None, None),
        P(("gx", "gy"), None, None),
        P(("gx", "gy"), None),
        P(("gx", "gy"), None),
        P(("gx", "gy")),
        P(("gx", "gy")),
        P(),
        P(),
    )
    out_specs = (P(("gx", "gy"), None, None), P(("gx", "gy"), None, None), P("gy", None, None))
    return jax.shard_map(local, mesh=mesh, in_specs=in_specs, out_specs=out_specs, check_vma=False)
```
